32 devices in a mesh: dp: 4 (over y, x), tm: 4 (over z), rows: 2 (over core).
Axes of the slice: x: 2, y: 2, z: 4, core: 2. Of those that a mesh axis runs over, the one named last changes fastest.
Arguments:
- latents: bfloat16 [4, 8, 8, 32, 384], P('dp', 'tm', 'rows'), may hold values from -6 to 6
- hidden: bfloat16 [4, 8, 8, 32, 384], P('dp', 'tm', 'rows'), may hold values from -8 to 8
- cotangent: bfloat16 [4, 8, 8, 32, 384], P('dp', 'tm', 'rows'), may hold values from -6 to 6
- conv_one: bfloat16 [3, 3, 3, 384, 384], replicated, may hold values from -0.0625 to 0.0625
- conv_two: bfloat16 [3, 3, 3, 384, 384], replicated, may hold values from -0.0625 to 0.0625
- lengths: int32 [4], P('dp'), may hold values from 3 to 8, as said below
Outputs:
- latent_grad: float32 [4, 8, 8, 32, 384], P('dp', None, None, ('tm', 'rows'))
The draws below stay inside these ranges and needn't reach their ends.
Inputs may be any that keep to these rules, and one draw needn't show every extreme that they name: `lengths`: at least one clip has all 8 frames valid.
All inputs are finite; a program needn't handle non-finite values.
Results may differ from the reference program's by a relative error of at most 0.00092.
Values may be sent and summed in bfloat16 or wider, within the bound.
No kernel may reach another device: no remote copies, remote signals or barrier semaphores. Data moves between devices by JAX's collectives and lax.ppermute only.
A program may use at most 64 MiB of HBM per device.

```python
import jax
import jax.numpy as jnp
from jax import lax

C = 384
FRAME_DEV = 2
COLS = 32
FRAMES = 8
ROWS_ALL = 8
CLIPS = 4


def draw_lengths(key, part):
    drawn_counts = jax.random.randint(jax.random.fold_in(key, 11), (CLIPS,), FRAME_DEV + 1, FRAMES + 1)
    full_clip = jax.random.randint(jax.random.fold_in(key, 12), (), 0, CLIPS)
    return jnp.where(jnp.arange(CLIPS) == full_clip, FRAMES, drawn_counts).astype(jnp.int32)


def block_scale(key, extent, pieces, least, high):
    gain = 1.0
    for axis_at, blocks in pieces:
        heights = jax.random.uniform(jax.random.fold_in(jax.random.fold_in(key, 6), axis_at), (blocks,), jnp.float32, least / len(pieces), high / len(pieces))
        gain = gain * jnp.repeat(jnp.exp(heights), extent[axis_at] // blocks).reshape((-1,) + (1,) * (len(extent) - 1 - axis_at))
    return gain


def scatter_about(own_key, extent, deviation, bound, cuts=(), held_as=jnp.bfloat16):
    entries = jax.random.normal(own_key, extent, jnp.float32) * deviation
    if len(cuts) > 0:
        entries = block_scale(own_key, extent, cuts, -0.22, 0.18) * entries
    return jnp.clip(entries, min=-bound, max=bound).astype(held_as)


def setup_inputs(seed: int = 0) -> dict:
    key_list = jax.random.split(jax.random.key(seed), 7)
    return {
        "latents": scatter_about(key_list[0], (CLIPS, FRAMES, ROWS_ALL, COLS, C), 1.0, 6.0, ((0, 4), (1, 4), (2, 2))),
        "hidden": scatter_about(key_list[1], (CLIPS, FRAMES, ROWS_ALL, COLS, C), 2.0, 8.0, ((0, 4), (1, 4), (2, 2))),
        "cotangent": scatter_about(key_list[2], (CLIPS, FRAMES, ROWS_ALL, COLS, C), 1.0, 6.0, ((0, 4), (1, 4), (2, 2))),
        "conv_one": scatter_about(key_list[3], (3, 3, 3, C, C), (27 * C) ** -0.5, 0.0625),
        "conv_two": scatter_about(key_list[4], (3, 3, 3, C, C), (27 * C) ** -0.5, 0.0625),
        "lengths": draw_lengths(jax.random.fold_in(key_list[6], 71), 0),
    }


def silu_slope(values):
    sigmoid_of = jax.nn.sigmoid(values)
    return sigmoid_of * (1.0 + values * (1.0 - sigmoid_of))


def transposed(padded, kernel):
    flipped = jnp.flip(kernel, (0, 1, 2)).transpose(0, 1, 2, 4, 3)
    return lax.conv_general_dilated(padded, flipped, (1, 1, 1), "VALID", dimension_numbers=("NDHWC", "DHWIO", "NDHWC"), preferred_element_type=jnp.float32)


def reference(latents, hidden, cotangent, conv_one, conv_two, lengths):
    frames = jnp.arange(FRAMES, dtype=jnp.int32)
    live_frames = frames[None, :] < lengths[:, None]
    masked = jnp.where(live_frames[:, :, None, None, None], cotangent, jnp.zeros_like(cotangent))
    pad_spec = ((0, 0), (0, 2), (1, 1), (1, 1), (0, 0))
    grad_act = transposed(jnp.pad(masked, pad_spec), conv_two)
    grad_hidden = (grad_act * silu_slope(hidden.astype(jnp.float32))).astype(jnp.bfloat16)
    grad_input = transposed(jnp.pad(grad_hidden, pad_spec), conv_one)
    return masked.astype(jnp.float32) + grad_input * silu_slope(latents.astype(jnp.float32))
```

```python
import functools

import jax
import jax.numpy as jnp
from jax import lax
from jax.experimental import pallas as pl
from jax.experimental.pallas import tpu as pltpu
from jax.sharding import PartitionSpec as P

F32 = jnp.float32
BF16 = jnp.bfloat16
VMEM = pl.BlockSpec(memory_space=pltpu.VMEM)
SMEM = pl.BlockSpec(memory_space=pltpu.SMEM)
ANY = pl.BlockSpec(memory_space=pl.ANY)
LANES = 128


def lanes(channels):
    return [(at, slice(at * LANES, (at + 1) * LANES)) for at in range(channels // LANES)]


def pairing(count):
    if count & (count - 1) == 0:
        return [
            ([(i, i ^ s) for i in range(count)], lambda i, s=s: i ^ s, lambda i, s=s: i ^ s)
            for s in range(1, count)
        ]
    return [
        (
            [(i, (i + s) % count) for i in range(count)],
            lambda i, s=s: lax.rem(i + s, count),
            lambda i, s=s: lax.rem(i + count - s, count),
        )
        for s in range(1, count)
    ]


def silu_slope(values):
    sigmoid_of = jax.nn.sigmoid(values)
    return sigmoid_of * (1.0 + values * (1.0 - sigmoid_of))


def dot_last(a, b):
    return lax.dot_general(a, b, (((1,), (1,)), ((), ())), preferred_element_type=F32)


def pack_kernel(time_devs, halos, masked, *refs):
    count = len(halos)
    len_ref, ins = refs[0], refs[1 : 1 + count]
    outs, turned = refs[1 + count : -count], refs[-count:]
    me = lax.axis_index("tm")
    targets = [me] + [to(me) for _, to, _ in pairing(time_devs)]
    for at in range(count):
        ref, stage, halo = ins[at], turned[at], halos[at]
        frames, rows, cols, _ = ref.shape
        unit = frames * rows
        if halo:
            edge = jnp.zeros((stage.shape[0], halo * unit, LANES), F32)
            stage[:, 0 : halo * unit, :] = edge
            stage[:, (halo + cols) * unit :, :] = edge
        for frame in range(frames):
            for row in range(rows):
                value = ref[frame, row].astype(F32)
                if masked:
                    value = jnp.where(me * frames + frame < len_ref[0], value, 0.0)
                start = halo * unit + frame * rows + row
                for at_lane, lane in lanes(value.shape[1]):
                    stage[at_lane, pl.ds(start, cols, stride=unit), :] = value[:, lane]
        block = cols // time_devs
        size = (block + 2 * halo) * unit
        for step, target in enumerate(targets):
            start = pl.multiple_of(target * (block * unit), unit)
            for at_lane, lane in lanes(ref.shape[3]):
                outs[at * time_devs + step][:, lane] = stage[at_lane, pl.ds(start, size), :].astype(BF16)


def pack(arrays, lengths, halos, masked, time_devs):
    frames, rows, cols, channels = arrays[0].shape
    unit = frames * rows
    shapes = [
        jax.ShapeDtypeStruct(((cols // time_devs + 2 * halo) * unit, channels), BF16)
        for halo in halos
        for _ in range(time_devs)
    ]
    out = pl.pallas_call(
        functools.partial(pack_kernel, time_devs, halos, masked),
        out_shape=shapes,
        in_specs=[SMEM] + [VMEM] * len(arrays),
        out_specs=[VMEM] * len(shapes),
        scratch_shapes=[
            pltpu.VMEM((channels // LANES, (cols + 2 * halo) * unit, LANES), F32) for halo in halos
        ],
        compiler_params=pltpu.CompilerParams(vmem_limit_bytes=12 << 20),
        cost_estimate=pl.CostEstimate(flops=1000, bytes_accessed=2 << 20, transcendentals=0),
    )(lengths, *arrays)
    return [out[at * time_devs : (at + 1) * time_devs] for at in range(len(arrays))]


def gather_block(dims, wins, halo, stage, dest, col_stride, row_pad):
    time_devs, row_devs, frame_dev, row_dev, col_dev = dims
    frames = time_devs * frame_dev
    unit = frame_dev * row_dev
    tm, row_at = lax.axis_index("tm"), lax.axis_index("rows")
    from_tm = [tm] + [source(tm) for _, _, source in pairing(time_devs)]
    from_row = [row_at] + [source(row_at) for _, _, source in pairing(row_devs)]
    cols = col_dev + 2 * halo
    for s in range(time_devs):
        for q in range(row_devs):
            at = s * row_devs + q
            first = row_at * (col_dev * unit)
            for at_lane, lane in lanes(wins[at].shape[1]):
                slot = at * dest.shape[0] + at_lane
                stage[slot, 0 : wins[at].shape[0], :] = wins[at][:, lane].astype(F32)
                for frame in range(frame_dev):
                    for row in range(row_dev):
                        start = first + frame * row_dev + row
                        target = (
                            (from_row[q] * row_dev + row + row_pad) * frames
                            + from_tm[s] * frame_dev
                            + frame
                        )
                        dest[at_lane, pl.ds(target, cols, stride=col_stride), :] = stage[
                            slot, pl.ds(start, cols, stride=unit), :
                        ]


def spread(full, shifts, cols, rows, frames):
    size = cols * (rows + 2) * frames
    place = lax.rem(lax.broadcasted_iota(jnp.int32, (size, LANES), 0), frames)
    for a in range(3):
        for p in range(2):
            count = size - p * frames
            for at_lane, lane in lanes(shifts.shape[3]):
                value = full[at_lane, pl.ds(a + p * frames, count), :]
                value = jnp.where(place[:count] < frames - a, value, 0.0).astype(BF16)
                shifts[a, p, 0:count, lane] = value


def tap(shifts, a, r, c, cols, rows, frames):
    parity = r % 2
    start = (r - parity) * frames
    pitch = (rows + 2) * frames
    return jnp.concatenate(
        [
            shifts[a, parity, (c + w) * pitch + start : (c + w) * pitch + start + rows * frames, :]
            for w in range(cols)
        ],
        axis=0,
    )


def taps_of(shifts, weights, a, cols, rows, frames):
    order = [(r, c) for r in range(3) for c in range(3)]
    moved = jnp.concatenate([tap(shifts, a, r, c, cols, rows, frames) for r, c in order], axis=1)
    mixed = jnp.concatenate([weights[a, 2 - r, 2 - c] for r, c in order], axis=1)
    return moved, mixed


def weight_copies(source, buffer, sems):
    return [pltpu.make_async_copy(source.at[2 - a], buffer.at[a], sems.at[a]) for a in range(3)]


def first_kernel(dims, count, *refs):
    wins, weight_ref = refs[:count], refs[count]
    acc_ref, mid_ref = refs[count + 1 : count + 3]
    stage, full, shifts, buffer, sems = refs[count + 3 :]
    time_devs, row_devs, frame_dev, row_dev, col_dev = dims
    frames, rows = time_devs * frame_dev, row_devs * row_dev
    copies = weight_copies(weight_ref, buffer, sems)
    for copy in copies:
        copy.start()
    full[...] = jnp.zeros_like(full)
    pitch = (rows + 2) * frames
    gather_block(dims, wins, 2, stage, full, pitch, 1)
    spread(full, shifts, col_dev + 4, rows, frames)
    plane = rows * frames
    for w in range(col_dev):
        start = (w + 2) * pitch + frames
        mid_ref[:, w * plane : (w + 1) * plane, :] = full[:, start : start + plane, :]
    acc_ref[...] = jnp.zeros_like(acc_ref)

    @pl.loop(0, 3)
    def _(a):
        pltpu.make_async_copy(weight_ref.at[2 - a], buffer.at[a], sems.at[a]).wait()
        moved, mixed = taps_of(shifts, buffer, a, col_dev + 2, rows, frames)
        acc_ref[...] += dot_last(moved, mixed)


def second_kernel(dims, count, cols_all, *refs):
    hid, lat = refs[:count], refs[count : 2 * count]
    acc_ref, mid_ref, weight_ref = refs[2 * count : 2 * count + 3]
    out_ref = refs[2 * count + 3]
    stage, slopes, full, shifts, acc, buffer, sems = refs[2 * count + 4 :]
    time_devs, row_devs, frame_dev, row_dev, col_dev = dims
    frames, rows = time_devs * frame_dev, row_devs * row_dev
    copies = weight_copies(weight_ref, buffer, sems)
    for copy in copies:
        copy.start()
    plane, pitch = rows * frames, (rows + 2) * frames
    gather_block(dims, hid, 1, stage, slopes, plane, 0)
    full[...] = jnp.zeros_like(full)
    first_col = (lax.axis_index("tm") * row_devs + lax.axis_index("rows")) * col_dev - 1
    for w in range(col_dev + 2):
        col = first_col + w
        inside = jnp.logical_and(col >= 0, col < cols_all)
        here = slice(w * plane, (w + 1) * plane)
        start = w * pitch + frames
        for at_lane, lane in lanes(acc_ref.shape[1]):
            value = acc_ref[here, lane] * silu_slope(slopes[at_lane, here, :])
            full[at_lane, start : start + plane, :] = jnp.where(inside, value, 0.0)
    spread(full, shifts, col_dev + 2, rows, frames)
    acc[...] = jnp.zeros_like(acc)

    @pl.loop(0, 3)
    def _(a):
        pltpu.make_async_copy(weight_ref.at[2 - a], buffer.at[a], sems.at[a]).wait()
        moved, mixed = taps_of(shifts, buffer, a, col_dev, rows, frames)
        acc[...] += dot_last(mixed, moved)

    gather_block(dims, lat, 0, stage, slopes, plane, 0)
    size = col_dev * plane
    for at_lane, lane in lanes(acc.shape[0]):
        full[at_lane, 0:size, :] = mid_ref[at_lane] + acc[lane, :].T * silu_slope(
            slopes[at_lane, 0:size, :]
        )
        for frame in range(frames):
            for row in range(rows):
                out_ref[0, frame, row, :, lane] = full[
                    at_lane, pl.ds(row * frames + frame, col_dev, stride=plane), :
                ]


def on_device(latents, hidden, cotangent, conv_one, conv_two, lengths):
    _, frame_dev, row_dev, cols, channels = latents.shape
    time_devs, row_devs = lax.axis_size("tm"), lax.axis_size("rows")
    col_dev = cols // (time_devs * row_devs)
    frames, rows = time_devs * frame_dev, row_devs * row_dev
    unit = frame_dev * row_dev
    dims = (time_devs, row_devs, frame_dev, row_dev, col_dev)
    count = time_devs * row_devs

    def over_tm(windows):
        return [windows[0]] + [
            lax.ppermute(windows[step + 1], "tm", pairs)
            for step, (pairs, _, _) in enumerate(pairing(time_devs))
        ]

    def over_rows(windows):
        out = []
        for window in windows:
            out.append(window)
            out += [lax.ppermute(window, "rows", pairs) for pairs, _, _ in pairing(row_devs)]
        return out

    (cot,) = pack([cotangent[0]], lengths, (2,), True, time_devs)
    hid, lat = pack([hidden[0], latents[0]], lengths, (1, 0), False, time_devs)
    cot = over_rows(over_tm(cot))
    hid = over_rows(over_tm(hid))
    lat = over_rows(over_tm(lat))

    plane, pitch = rows * frames, (rows + 2) * frames
    chip, parts = cols // time_devs, channels // LANES

    def scratch(halo):
        return [
            pltpu.VMEM((count * parts, (chip + 2 * halo) * unit, LANES), F32),
        ]

    acc, mid = pl.pallas_call(
        functools.partial(first_kernel, dims, count),
        out_shape=[
            jax.ShapeDtypeStruct(((col_dev + 2) * plane, channels), F32),
            jax.ShapeDtypeStruct((parts, col_dev * plane, LANES), F32),
        ],
        in_specs=[VMEM] * count + [ANY],
        out_specs=[VMEM] * 2,
        scratch_shapes=scratch(2)
        + [
            pltpu.VMEM((parts, (col_dev + 4) * pitch + frames, LANES), F32),
            pltpu.VMEM((3, 2, (col_dev + 4) * pitch, channels), BF16),
            pltpu.VMEM((3,) + conv_two.shape[1:], BF16),
            pltpu.SemaphoreType.DMA((3,)),
        ],
        compiler_params=pltpu.CompilerParams(vmem_limit_bytes=32 << 20),
        cost_estimate=pl.CostEstimate(
            flops=2 * 27 * (col_dev + 2) * plane * channels * channels,
            bytes_accessed=10 << 20,
            transcendentals=0,
        ),
    )(*cot, conv_two)
    return pl.pallas_call(
        functools.partial(second_kernel, dims, count, cols),
        out_shape=jax.ShapeDtypeStruct((1, frames, rows, col_dev, channels), F32),
        in_specs=[VMEM] * (2 * count + 2) + [ANY],
        out_specs=VMEM,
        scratch_shapes=scratch(1)
        + [
            pltpu.VMEM((parts, (col_dev + 2) * plane, LANES), F32),
            pltpu.VMEM((parts, (col_dev + 2) * pitch + frames, LANES), F32),
            pltpu.VMEM((3, 2, (col_dev + 2) * pitch, channels), BF16),
            pltpu.VMEM((channels, col_dev * plane), F32),
            pltpu.VMEM((3,) + conv_one.shape[1:], BF16),
            pltpu.SemaphoreType.DMA((3,)),
        ],
        compiler_params=pltpu.CompilerParams(vmem_limit_bytes=32 << 20),
        cost_estimate=pl.CostEstimate(
            flops=2 * 27 * col_dev * plane * channels * channels,
            bytes_accessed=10 << 20,
            transcendentals=0,
        ),
    )(*hid, *lat, acc, mid, conv_one)


def solution(mesh):
    spec = P("dp", "tm", "rows", None, None)
    return jax.shard_map(
        on_device,
        mesh=mesh,
        in_specs=(spec, spec, spec, P(), P(), P("dp")),
        out_specs=P("dp", None, None, ("tm", "rows"), None),
        check_vma=False,
    )
```

```python
import functools

import jax
import jax.numpy as jnp
from jax import lax
from jax.experimental import pallas as pl
from jax.experimental.pallas import tpu as pltpu
from jax.sharding import PartitionSpec as P


F32 = jnp.float32
BF16 = jnp.bfloat16
VMEM = pl.BlockSpec(memory_space=pltpu.VMEM)
SMEM = pl.BlockSpec(memory_space=pltpu.SMEM)
HBM = pl.BlockSpec(memory_space=pltpu.HBM)
LANES = 128


def lanes(channels):
    return [(at, slice(at * LANES, (at + 1) * LANES)) for at in range(channels // LANES)]


def pairing(count):
    if count & (count - 1) == 0:
        return [
            ([(i, i ^ s) for i in range(count)], lambda i, s=s: i ^ s, lambda i, s=s: i ^ s)
            for s in range(1, count)
        ]
    return [
        (
            [(i, (i + s) % count) for i in range(count)],
            lambda i, s=s: lax.rem(i + s, count),
            lambda i, s=s: lax.rem(i + count - s, count),
        )
        for s in range(1, count)
    ]


def silu_slope(values):
    sigmoid_of = jax.nn.sigmoid(values)
    return sigmoid_of * (1.0 + values * (1.0 - sigmoid_of))


def dot_last(a, b):
    return lax.dot_general(a, b, (((1,), (1,)), ((), ())), preferred_element_type=F32)


def pack_kernel(time_devs, halos, masked, *refs):
    count = len(halos)
    len_ref, ins = refs[0], refs[1 : 1 + count]
    outs, turned = refs[1 + count : -count], refs[-count:]
    me = lax.axis_index("tm")
    targets = [me] + [to(me) for _, to, _ in pairing(time_devs)]
    for at in range(count):
        ref, stage, halo = ins[at], turned[at], halos[at]
        frames, rows, cols, _ = ref.shape
        unit = frames * rows
        if halo:
            edge = jnp.zeros((stage.shape[0], halo * unit, LANES), F32)
            stage[:, 0 : halo * unit, :] = edge
            stage[:, (halo + cols) * unit :, :] = edge
        for frame in range(frames):
            for row in range(rows):
                value = ref[frame, row].astype(F32)
                if masked:
                    value = jnp.where(me * frames + frame < len_ref[0], value, 0.0)
                start = halo * unit + frame * rows + row
                for at_lane, lane in lanes(value.shape[1]):
                    stage[at_lane, pl.ds(start, cols, stride=unit), :] = value[:, lane]
        block = cols // time_devs
        size = (block + 2 * halo) * unit
        for step, target in enumerate(targets):
            start = pl.multiple_of(target * (block * unit), unit)
            for at_lane, lane in lanes(ref.shape[3]):
                outs[at * time_devs + step][:, lane] = stage[at_lane, pl.ds(start, size), :].astype(BF16)


def pack(arrays, lengths, halos, masked, time_devs):
    frames, rows, cols, channels = arrays[0].shape
    unit = frames * rows
    shapes = [
        jax.ShapeDtypeStruct(((cols // time_devs + 2 * halo) * unit, channels), BF16)
        for halo in halos
        for _ in range(time_devs)
    ]
    out = pl.pallas_call(
        functools.partial(pack_kernel, time_devs, halos, masked),
        out_shape=shapes,
        in_specs=[SMEM] + [VMEM] * len(arrays),
        out_specs=[VMEM] * len(shapes),
        scratch_shapes=[
            pltpu.VMEM((channels // LANES, (cols + 2 * halo) * unit, LANES), F32) for halo in halos
        ],
        compiler_params=pltpu.CompilerParams(vmem_limit_bytes=12 << 20),
        cost_estimate=pl.CostEstimate(flops=6 * 10**9, bytes_accessed=2 << 20, transcendentals=0),
    )(lengths, *arrays)
    return [out[at * time_devs : (at + 1) * time_devs] for at in range(len(arrays))]


def gather_block(dims, wins, halo, stage, dest, col_stride, row_pad):
    time_devs, row_devs, frame_dev, row_dev, col_dev = dims
    frames = time_devs * frame_dev
    unit = frame_dev * row_dev
    tm, row_at = lax.axis_index("tm"), lax.axis_index("rows")
    from_tm = [tm] + [source(tm) for _, _, source in pairing(time_devs)]
    from_row = [row_at] + [source(row_at) for _, _, source in pairing(row_devs)]
    cols = col_dev + 2 * halo
    for s in range(time_devs):
        for q in range(row_devs):
            at = s * row_devs + q
            first = row_at * (col_dev * unit)
            for at_lane, lane in lanes(wins[at].shape[1]):
                slot = at * dest.shape[0] + at_lane
                stage[slot, 0 : wins[at].shape[0], :] = wins[at][:, lane].astype(F32)
                for frame in range(frame_dev):
                    for row in range(row_dev):
                        start = first + frame * row_dev + row
                        target = (
                            (from_row[q] * row_dev + row + row_pad) * frames
                            + from_tm[s] * frame_dev
                            + frame
                        )
                        dest[at_lane, pl.ds(target, cols, stride=col_stride), :] = stage[
                            slot, pl.ds(start, cols, stride=unit), :
                        ]


def spread(full, targets, cols, rows, frames):
    size = cols * (rows + 2) * frames
    place = lax.rem(lax.broadcasted_iota(jnp.int32, (size, LANES), 0), frames)
    for a, target in enumerate(targets):
        for p in range(2):
            count = size - p * frames
            for at_lane, lane in lanes(target.shape[2]):
                value = full[at_lane, pl.ds(a + p * frames, count), :]
                value = jnp.where(place[:count] < frames - a, value, 0.0).astype(BF16)
                target[p, 0:count, lane] = value


def tap(shifts, r, c, cols, rows, frames):
    parity = r % 2
    start = (r - parity) * frames
    pitch = (rows + 2) * frames
    return jnp.concatenate(
        [
            shifts[parity, (c + w) * pitch + start : (c + w) * pitch + start + rows * frames, :]
            for w in range(cols)
        ],
        axis=0,
    )


def taps_of(shifts, weights, cols, rows, frames):
    order = [(r, c) for r in range(3) for c in range(3)]
    moved = jnp.concatenate([tap(shifts, r, c, cols, rows, frames) for r, c in order], axis=1)
    mixed = jnp.concatenate([weights[2 - r, 2 - c] for r, c in order], axis=1)
    return moved, mixed


def chunk_copy(source, at, target, sem):
    return pltpu.make_async_copy(source.at[2 - at], target, sem)


def first_kernel(dims, count, *refs):
    wins, weight_ref = refs[:count], refs[count]
    acc_ref, mid_ref, last_ref, next_ref = refs[count + 1 : count + 5]
    stage, full, shifts, buffer, sems = refs[count + 5 :]
    time_devs, row_devs, frame_dev, row_dev, col_dev = dims
    frames, rows = time_devs * frame_dev, row_devs * row_dev
    for a in range(2):
        chunk_copy(weight_ref, a, buffer.at[a], sems.at[a]).start()
    chunk_copy(weight_ref, 2, next_ref, sems.at[2]).start()
    full[...] = jnp.zeros_like(full)
    plane, pitch = rows * frames, (rows + 2) * frames
    gather_block(dims, wins, 2, stage, full, pitch, 1)
    spread(full, [shifts.at[0], shifts.at[1], last_ref], col_dev + 4, rows, frames)
    for w in range(col_dev):
        start = (w + 2) * pitch + frames
        mid_ref[:, w * plane : (w + 1) * plane, :] = full[:, start : start + plane, :]
    acc_ref[...] = jnp.zeros_like(acc_ref)

    @pl.loop(0, 2)
    def _(a):
        chunk_copy(weight_ref, a, buffer.at[a], sems.at[a]).wait()
        moved, mixed = taps_of(shifts.at[a], buffer.at[a], col_dev + 2, rows, frames)
        acc_ref[...] += dot_last(moved, mixed)

    chunk_copy(weight_ref, 2, next_ref, sems.at[2]).wait()


def last_tap_kernel(dims, acc_in, shifts, weights, acc_ref):
    time_devs, row_devs, frame_dev, row_dev, col_dev = dims
    frames, rows = time_devs * frame_dev, row_devs * row_dev
    moved, mixed = taps_of(shifts, weights, col_dev + 2, rows, frames)
    acc_ref[...] = acc_in[...] + dot_last(moved, mixed)


def second_kernel(dims, count, cols_all, *refs):
    hid = refs[:count]
    acc_ref, weight_ref, out_ref = refs[count : count + 3]
    stage, slopes, full, shifts, buffer, sems = refs[count + 3 :]
    time_devs, row_devs, frame_dev, row_dev, col_dev = dims
    frames, rows = time_devs * frame_dev, row_devs * row_dev
    for a in range(3):
        chunk_copy(weight_ref, a, buffer.at[a], sems.at[a]).start()
    plane, pitch = rows * frames, (rows + 2) * frames
    gather_block(dims, hid, 1, stage, slopes, plane, 0)
    full[...] = jnp.zeros_like(full)
    first_col = (lax.axis_index("tm") * row_devs + lax.axis_index("rows")) * col_dev - 1
    for w in range(col_dev + 2):
        col = first_col + w
        inside = jnp.logical_and(col >= 0, col < cols_all)
        here = slice(w * plane, (w + 1) * plane)
        start = w * pitch + frames
        for at_lane, lane in lanes(acc_ref.shape[1]):
            value = acc_ref[here, lane] * silu_slope(slopes[at_lane, here, :])
            full[at_lane, start : start + plane, :] = jnp.where(inside, value, 0.0)
    spread(full, [shifts.at[a] for a in range(3)], col_dev + 2, rows, frames)
    out_ref[...] = jnp.zeros_like(out_ref)

    @pl.loop(0, 3)
    def _(a):
        chunk_copy(weight_ref, a, buffer.at[a], sems.at[a]).wait()
        moved, mixed = taps_of(shifts.at[a], buffer.at[a], col_dev, rows, frames)
        out_ref[...] += dot_last(mixed, moved)


def final_kernel(dims, count, *refs):
    lat = refs[:count]
    acc_ref, mid_ref, out_ref, stage, slopes, full = refs[count:]
    time_devs, row_devs, frame_dev, row_dev, col_dev = dims
    frames, rows = time_devs * frame_dev, row_devs * row_dev
    plane = rows * frames
    gather_block(dims, lat, 0, stage, slopes, plane, 0)
    for at_lane, lane in lanes(acc_ref.shape[0]):
        full[at_lane] = mid_ref[at_lane] + acc_ref[lane, :].T * silu_slope(slopes[at_lane])
        for frame in range(frames):
            for row in range(rows):
                out_ref[0, frame, row, :, lane] = full[
                    at_lane, pl.ds(row * frames + frame, col_dev, stride=plane), :
                ]


def kernel_call(body, out_shape, in_specs, scratch, flops, room=24):
    return pl.pallas_call(
        body,
        out_shape=out_shape,
        in_specs=in_specs,
        out_specs=jax.tree.map(lambda _: VMEM, out_shape),
        scratch_shapes=scratch,
        compiler_params=pltpu.CompilerParams(vmem_limit_bytes=room << 20),
        cost_estimate=pl.CostEstimate(flops=flops, bytes_accessed=4 << 20, transcendentals=0),
    )


def on_device(latents, hidden, cotangent, conv_one, conv_two, lengths):
    _, frame_dev, row_dev, cols, channels = latents.shape
    time_devs, row_devs = lax.axis_size("tm"), lax.axis_size("rows")
    col_dev = cols // (time_devs * row_devs)
    frames, rows = time_devs * frame_dev, row_devs * row_dev
    unit = frame_dev * row_dev
    dims = (time_devs, row_devs, frame_dev, row_dev, col_dev)
    count = time_devs * row_devs
    plane, pitch = rows * frames, (rows + 2) * frames
    chip, parts = cols // time_devs, channels // LANES

    def over_tm(windows):
        out = [windows[0]]
        for step, (pairs, _, _) in enumerate(pairing(time_devs)):
            out.append(lax.ppermute(windows[step + 1], "tm", pairs))
        return out

    def over_rows(windows):
        out = []
        for window in windows:
            out.append(window)
            for pairs, _, _ in pairing(row_devs):
                out.append(lax.ppermute(window, "rows", pairs))
        return out

    def stage(halo):
        return pltpu.VMEM((count * parts, (chip + 2 * halo) * unit, LANES), F32)

    def part_rows(size):
        return pltpu.VMEM((parts, size, LANES), F32)

    mac = 2 * 9 * channels * channels
    wide, narrow = (col_dev + 2) * plane, col_dev * plane
    chunk = jax.ShapeDtypeStruct(conv_two.shape[1:], BF16)
    acc_shape = jax.ShapeDtypeStruct((wide, channels), F32)
    (cot,) = pack([cotangent[0]], lengths, (2,), True, time_devs)
    cot = over_rows(over_tm(cot))
    hid, lat = pack([hidden[0], latents[0]], lengths, (1, 0), False, time_devs)
    hid = over_rows(over_tm(hid))
    lat = over_rows(over_tm(lat))
    acc, mid, shifted, weights = kernel_call(
        functools.partial(first_kernel, dims, count),
        [
            acc_shape,
            jax.ShapeDtypeStruct((parts, narrow, LANES), F32),
            jax.ShapeDtypeStruct((2, (col_dev + 4) * pitch, channels), BF16),
            chunk,
        ],
        [VMEM] * count + [HBM],
        [
            stage(2),
            part_rows((col_dev + 4) * pitch + frames),
            pltpu.VMEM((2, 2, (col_dev + 4) * pitch, channels), BF16),
            pltpu.VMEM((2,) + chunk.shape, BF16),
            pltpu.SemaphoreType.DMA((3,)),
        ],
        2 * mac * wide,
    )(*cot, conv_two)
    acc = kernel_call(
        functools.partial(last_tap_kernel, dims), acc_shape, [VMEM] * 3, [], mac * wide
    )(acc, shifted, weights)
    grad = kernel_call(
        functools.partial(second_kernel, dims, count, cols),
        jax.ShapeDtypeStruct((channels, narrow), F32),
        [VMEM] * (count + 1) + [HBM],
        [
            stage(1),
            part_rows(wide),
            part_rows((col_dev + 2) * pitch + frames),
            pltpu.VMEM((3, 2, (col_dev + 2) * pitch, channels), BF16),
            pltpu.VMEM((3,) + chunk.shape, BF16),
            pltpu.SemaphoreType.DMA((3,)),
        ],
        3 * mac * narrow,
    )(*hid, acc, conv_one)
    return kernel_call(
        functools.partial(final_kernel, dims, count),
        jax.ShapeDtypeStruct((1, frames, rows, col_dev, channels), F32),
        [VMEM] * (count + 2),
        [stage(0), part_rows(narrow), part_rows(narrow)],
        1000000,
    )(*lat, grad, mid)


def solution(mesh):
    spec = P("dp", "tm", "rows", None, None)
    return jax.shard_map(
        on_device,
        mesh=mesh,
        in_specs=(spec, spec, spec, P(), P(), P("dp")),
        out_specs=P("dp", None, None, ("tm", "rows"), None),
        check_vma=False,
    )
```

```python
import functools

import jax
import jax.numpy as jnp
from jax import lax
from jax.experimental import pallas as pl
from jax.experimental.pallas import tpu as pltpu
from jax.sharding import PartitionSpec as P


F32 = jnp.float32
BF16 = jnp.bfloat16
VMEM = pl.BlockSpec(memory_space=pltpu.VMEM)
SMEM = pl.BlockSpec(memory_space=pltpu.SMEM)
HBM = pl.BlockSpec(memory_space=pltpu.HBM)
LANES = 128
STEPS = {4: (2, 3, 1)}


def lanes(channels):
    return [(at, slice(at * LANES, (at + 1) * LANES)) for at in range(channels // LANES)]


def pairing(count):
    if count & (count - 1) == 0:
        return [
            ([(i, i ^ s) for i in range(count)], lambda i, s=s: i ^ s, lambda i, s=s: i ^ s)
            for s in STEPS.get(count, range(1, count))
        ]
    return [
        (
            [(i, (i + s) % count) for i in range(count)],
            lambda i, s=s: lax.rem(i + s, count),
            lambda i, s=s: lax.rem(i + count - s, count),
        )
        for s in range(1, count)
    ]


def silu_slope(values):
    sigmoid_of = jax.nn.sigmoid(values)
    return sigmoid_of * (1.0 + values * (1.0 - sigmoid_of))


def dot_last(a, b):
    return lax.dot_general(a, b, (((1,), (1,)), ((), ())), preferred_element_type=F32)


def window_rows(halos, unit, block):
    ends = [0]
    for halo in halos:
        ends.append(ends[-1] + (block + 2 * halo) * unit)
    return ends


def pack_kernel(time_devs, halos, masked, *refs):
    count = len(halos)
    len_ref, ins = refs[0], refs[1 : 1 + count]
    outs, turned = refs[1 + count : -count], refs[-count:]
    me = lax.axis_index("tm")
    targets = [me] + [to(me) for _, to, _ in pairing(time_devs)]
    frames, rows, cols, channels = ins[0].shape
    unit, block = frames * rows, cols // time_devs
    ends = window_rows(halos, unit, block)
    for at in range(count):
        ref, stage, halo = ins[at], turned[at], halos[at]
        if halo:
            edge = jnp.zeros((stage.shape[0], halo * unit, LANES), F32)
            stage[:, 0 : halo * unit, :] = edge
            stage[:, (halo + cols) * unit :, :] = edge
        for frame in range(frames):
            for row in range(rows):
                value = ref[frame, row].astype(F32)
                if masked:
                    value = jnp.where(me * frames + frame < len_ref[0], value, 0.0)
                start = halo * unit + frame * rows + row
                for at_lane, lane in lanes(channels):
                    stage[at_lane, pl.ds(start, cols, stride=unit), :] = value[:, lane]
        size = ends[at + 1] - ends[at]
        for step, target in enumerate(targets):
            start = pl.multiple_of(target * (block * unit), unit)
            for at_lane, lane in lanes(channels):
                outs[step][ends[at] : ends[at + 1], lane] = stage[
                    at_lane, pl.ds(start, size), :
                ].astype(BF16)


def pack(arrays, lengths, halos, masked, time_devs):
    frames, rows, cols, channels = arrays[0].shape
    unit = frames * rows
    size = window_rows(halos, unit, cols // time_devs)[-1]
    return pl.pallas_call(
        functools.partial(pack_kernel, time_devs, halos, masked),
        out_shape=[jax.ShapeDtypeStruct((size, channels), BF16)] * time_devs,
        in_specs=[SMEM] + [VMEM] * len(arrays),
        out_specs=[VMEM] * time_devs,
        scratch_shapes=[
            pltpu.VMEM((channels // LANES, (cols + 2 * halo) * unit, LANES), F32) for halo in halos
        ],
        compiler_params=pltpu.CompilerParams(vmem_limit_bytes=12 << 20),
        cost_estimate=pl.CostEstimate(
            flops=6 * 10**9, bytes_accessed=2 << 20, transcendentals=0
        ),
    )(lengths, *arrays)


def gather_block(dims, wins, halo, begin, stage, dest, col_stride, row_pad):
    time_devs, row_devs, frame_dev, row_dev, col_dev = dims
    frames = time_devs * frame_dev
    unit = frame_dev * row_dev
    tm, row_at = lax.axis_index("tm"), lax.axis_index("rows")
    from_tm = [tm] + [source(tm) for _, _, source in pairing(time_devs)]
    from_row = [row_at] + [source(row_at) for _, _, source in pairing(row_devs)]
    cols = col_dev + 2 * halo
    for s in range(time_devs):
        for q in range(row_devs):
            at = s * row_devs + q
            first = row_at * (col_dev * unit)
            for at_lane, lane in lanes(wins[at].shape[1]):
                slot = at * dest.shape[0] + at_lane
                size = stage.shape[1]
                stage[slot] = wins[at][begin : begin + size, lane].astype(F32)
                for frame in range(frame_dev):
                    for row in range(row_dev):
                        start = first + frame * row_dev + row
                        target = (
                            (from_row[q] * row_dev + row + row_pad) * frames
                            + from_tm[s] * frame_dev
                            + frame
                        )
                        dest[at_lane, pl.ds(target, cols, stride=col_stride), :] = stage[
                            slot, pl.ds(start, cols, stride=unit), :
                        ]


def spread(full, targets, cols, rows, frames):
    size = cols * (rows + 2) * frames
    place = lax.rem(lax.broadcasted_iota(jnp.int32, (size, LANES), 0), frames)
    for a, target in enumerate(targets):
        for p in range(2):
            count = size - p * frames
            for at_lane, lane in lanes(target.shape[2]):
                value = full[at_lane, pl.ds(a + p * frames, count), :]
                value = jnp.where(place[:count] < frames - a, value, 0.0).astype(BF16)
                target[p, 0:count, lane] = value


def tap(shifts, r, c, cols, rows, frames):
    parity = r % 2
    start = (r - parity) * frames
    pitch = (rows + 2) * frames
    return jnp.concatenate(
        [
            shifts[parity, (c + w) * pitch + start : (c + w) * pitch + start + rows * frames, :]
            for w in range(cols)
        ],
        axis=0,
    )


def taps_of(shifts, weights, cols, rows, frames):
    order = [(r, c) for r in range(3) for c in range(3)]
    moved = jnp.concatenate([tap(shifts, r, c, cols, rows, frames) for r, c in order], axis=1)
    mixed = jnp.concatenate([weights[2 - r, 2 - c] for r, c in order], axis=1)
    return moved, mixed


def first_kernel(dims, count, *refs):
    wins, weight_ref = refs[:count], refs[count]
    acc_ref, mid_ref = refs[count + 1 : count + 3]
    stage, full, shifts = refs[count + 3 :]
    time_devs, row_devs, frame_dev, row_dev, col_dev = dims
    frames, rows = time_devs * frame_dev, row_devs * row_dev
    full[...] = jnp.zeros_like(full)
    plane, pitch = rows * frames, (rows + 2) * frames
    gather_block(dims, wins, 2, 0, stage, full, pitch, 1)
    spread(full, [shifts.at[0], shifts.at[1], shifts.at[2]], col_dev + 4, rows, frames)
    for w in range(col_dev):
        start = (w + 2) * pitch + frames
        mid_ref[:, w * plane : (w + 1) * plane, :] = full[:, start : start + plane, :]
    acc_ref[...] = jnp.zeros_like(acc_ref)

    @pl.loop(0, 3)
    def _(a):
        moved, mixed = taps_of(shifts.at[a], weight_ref.at[2 - a], col_dev + 2, rows, frames)
        acc_ref[...] += dot_last(moved, mixed)


def second_kernel(dims, count, cols_all, *refs):
    wins = refs[:count]
    acc_ref, mid_ref, weight_ref, out_ref = refs[count : count + 4]
    stage, late, slopes, full, shifts, grad = refs[count + 4 :]
    time_devs, row_devs, frame_dev, row_dev, col_dev = dims
    frames, rows = time_devs * frame_dev, row_devs * row_dev
    plane, pitch = rows * frames, (rows + 2) * frames
    gather_block(dims, wins, 1, 0, stage, slopes, plane, 0)
    full[...] = jnp.zeros_like(full)
    first_col = (lax.axis_index("tm") * row_devs + lax.axis_index("rows")) * col_dev - 1
    for w in range(col_dev + 2):
        col = first_col + w
        inside = jnp.logical_and(col >= 0, col < cols_all)
        here = slice(w * plane, (w + 1) * plane)
        start = w * pitch + frames
        for at_lane, lane in lanes(acc_ref.shape[1]):
            value = acc_ref[here, lane] * silu_slope(slopes[at_lane, here, :])
            full[at_lane, start : start + plane, :] = jnp.where(inside, value, 0.0)
    spread(full, [shifts.at[a] for a in range(3)], col_dev + 2, rows, frames)
    grad[...] = jnp.zeros_like(grad)

    @pl.loop(0, 3)
    def _(a):
        moved, mixed = taps_of(shifts.at[a], weight_ref.at[2 - a], col_dev, rows, frames)
        grad[...] += dot_last(mixed, moved)

    gather_block(dims, wins, 0, stage.shape[1], late, slopes, plane, 0)
    size = col_dev * plane
    for at_lane, lane in lanes(grad.shape[0]):
        full[at_lane, 0:size, :] = mid_ref[at_lane] + grad[lane, :].T * silu_slope(
            slopes[at_lane, 0:size, :]
        )
        for frame in range(frames):
            for row in range(rows):
                out_ref[0, frame, row, :, lane] = full[
                    at_lane, pl.ds(row * frames + frame, col_dev, stride=plane), :
                ]


def kernel_call(body, out_shape, in_specs, scratch, flops, room=24):
    return pl.pallas_call(
        body,
        out_shape=out_shape,
        in_specs=in_specs,
        out_specs=jax.tree.map(lambda _: VMEM, out_shape),
        scratch_shapes=scratch,
        compiler_params=pltpu.CompilerParams(vmem_limit_bytes=room << 20),
        cost_estimate=pl.CostEstimate(flops=flops, bytes_accessed=4 << 20, transcendentals=0),
    )


def on_device(latents, hidden, cotangent, conv_one, conv_two, lengths):
    _, frame_dev, row_dev, cols, channels = latents.shape
    time_devs, row_devs = lax.axis_size("tm"), lax.axis_size("rows")
    col_dev = cols // (time_devs * row_devs)
    frames, rows = time_devs * frame_dev, row_devs * row_dev
    unit = frame_dev * row_dev
    dims = (time_devs, row_devs, frame_dev, row_dev, col_dev)
    count = time_devs * row_devs
    plane, pitch = rows * frames, (rows + 2) * frames
    chip, parts = cols // time_devs, channels // LANES

    def over_tm(windows):
        out = [windows[0]]
        for step, (pairs, _, _) in enumerate(pairing(time_devs)):
            out.append(lax.ppermute(windows[step + 1], "tm", pairs))
        return out

    def over_rows(windows):
        out = []
        for window in windows:
            out.append(window)
            for pairs, _, _ in pairing(row_devs):
                out.append(lax.ppermute(window, "rows", pairs))
        return out

    def stage(halo):
        return pltpu.VMEM((count * parts, (chip + 2 * halo) * unit, LANES), F32)

    def part_rows(size):
        return pltpu.VMEM((parts, size, LANES), F32)

    mac = 2 * 9 * channels * channels
    wide, narrow = (col_dev + 2) * plane, col_dev * plane
    acc_shape = jax.ShapeDtypeStruct((wide, channels), F32)
    cot = pack([cotangent[0]], lengths, (2,), True, time_devs)
    cot = over_rows(over_tm(cot))
    hid = pack([hidden[0], latents[0]], lengths, (1, 0), False, time_devs)
    hid = over_rows(over_tm(hid))
    acc, mid = kernel_call(
        functools.partial(first_kernel, dims, count),
        [acc_shape, jax.ShapeDtypeStruct((parts, narrow, LANES), F32)],
        [VMEM] * (count + 1),
        [
            stage(2),
            part_rows((col_dev + 4) * pitch + frames),
            pltpu.VMEM((3, 2, (col_dev + 4) * pitch, channels), BF16),
        ],
        3 * mac * wide,
    )(*cot, conv_two)
    return kernel_call(
        functools.partial(second_kernel, dims, count, cols),
        jax.ShapeDtypeStruct((1, frames, rows, col_dev, channels), F32),
        [VMEM] * (count + 3),
        [
            stage(1),
            stage(0),
            part_rows(wide),
            part_rows((col_dev + 2) * pitch + frames),
            pltpu.VMEM((3, 2, (col_dev + 2) * pitch, channels), BF16),
            pltpu.VMEM((channels, narrow), F32),
        ],
        3 * mac * narrow,
    )(*hid, acc, mid, conv_one)


def solution(mesh):
    spec = P("dp", "tm", "rows", None, None)
    return jax.shard_map(
        on_device,
        mesh=mesh,
        in_specs=(spec, spec, spec, P(), P(), P("dp")),
        out_specs=P("dp", None, None, ("tm", "rows"), None),
        check_vma=False,
    )
```

```python
import functools

import jax
import jax.numpy as jnp
from jax import lax
from jax.experimental import pallas as pl
from jax.experimental.pallas import tpu as pltpu
from jax.sharding import PartitionSpec as P


F32 = jnp.float32
BF16 = jnp.bfloat16
VMEM = pl.BlockSpec(memory_space=pltpu.VMEM)
SMEM = pl.BlockSpec(memory_space=pltpu.SMEM)
LANES = 128
STEPS = {4: (3, 2, 1)}


def lanes(channels):
    return [(at, slice(at * LANES, (at + 1) * LANES)) for at in range(channels // LANES)]


def pairing(count):
    if count & (count - 1) == 0:
        return [
            ([(i, i ^ s) for i in range(count)], lambda i, s=s: i ^ s, lambda i, s=s: i ^ s)
            for s in STEPS.get(count, range(1, count))
        ]
    return [
        (
            [(i, (i + s) % count) for i in range(count)],
            lambda i, s=s: lax.rem(i + s, count),
            lambda i, s=s: lax.rem(i + count - s, count),
        )
        for s in range(1, count)
    ]


def silu_slope(values):
    sigmoid_of = jax.nn.sigmoid(values)
    return sigmoid_of * (1.0 + values * (1.0 - sigmoid_of))


def dot_last(a, b):
    return lax.dot_general(a, b, (((1,), (1,)), ((), ())), preferred_element_type=F32)


def window_rows(halos, unit, block):
    ends = [0]
    for halo in halos:
        ends.append(ends[-1] + (block + 2 * halo) * unit)
    return ends


def pack_kernel(time_devs, halos, masked, *refs):
    count = len(halos)
    len_ref, ins = refs[0], refs[1 : 1 + count]
    outs, turned = refs[1 + count : -count], refs[-count:]
    me = lax.axis_index("tm")
    targets = [me] + [to(me) for _, to, _ in pairing(time_devs)]
    frames, rows, cols, channels = ins[0].shape
    unit, block = frames * rows, cols // time_devs
    ends = window_rows(halos, unit, block)
    for at in range(count):
        ref, stage, halo = ins[at], turned[at], halos[at]
        if halo:
            edge = jnp.zeros((stage.shape[0], halo * unit, LANES), F32)
            stage[:, 0 : halo * unit, :] = edge
            stage[:, (halo + cols) * unit :, :] = edge
        for frame in range(frames):
            for row in range(rows):
                value = ref[frame, row].astype(F32)
                if masked:
                    value = jnp.where(me * frames + frame < len_ref[0], value, 0.0)
                start = halo * unit + frame * rows + row
                for at_lane, lane in lanes(channels):
                    stage[at_lane, pl.ds(start, cols, stride=unit), :] = value[:, lane]
        size = ends[at + 1] - ends[at]
        for step, target in enumerate(targets):
            start = pl.multiple_of(target * (block * unit), unit)
            for at_lane, lane in lanes(channels):
                outs[step][ends[at] : ends[at + 1], lane] = stage[
                    at_lane, pl.ds(start, size), :
                ].astype(BF16)


def pack(arrays, lengths, halos, masked, time_devs):
    frames, rows, cols, channels = arrays[0].shape
    unit = frames * rows
    size = window_rows(halos, unit, cols // time_devs)[-1]
    return pl.pallas_call(
        functools.partial(pack_kernel, time_devs, halos, masked),
        out_shape=[jax.ShapeDtypeStruct((size, channels), BF16)] * time_devs,
        in_specs=[SMEM] + [VMEM] * len(arrays),
        out_specs=[VMEM] * time_devs,
        scratch_shapes=[
            pltpu.VMEM((channels // LANES, (cols + 2 * halo) * unit, LANES), F32) for halo in halos
        ],
        compiler_params=pltpu.CompilerParams(vmem_limit_bytes=12 << 20),
        cost_estimate=pl.CostEstimate(
            flops=6 * 10**9, bytes_accessed=2 << 20, transcendentals=0
        ),
    )(lengths, *arrays)


def laid_out(dims, wins, halo, begin, target, stage, dest):
    time_devs, _, frame_dev, row_dev, col_dev = dims
    frames, unit = time_devs * frame_dev, frame_dev * row_dev
    tm = lax.axis_index("tm")
    from_tm = [tm] + [source(tm) for _, _, source in pairing(time_devs)]
    cols = col_dev + 2 * halo
    first = pl.multiple_of(target * (col_dev * unit), unit)
    for s in range(time_devs):
        for at_lane, lane in lanes(wins[s].shape[1]):
            slot = s * stage.shape[0] // time_devs + at_lane
            stage[slot] = wins[s][begin : begin + stage.shape[1], lane].astype(F32)
            for frame in range(frame_dev):
                for row in range(row_dev):
                    start = first + frame * row_dev + row
                    place = row * frames + from_tm[s] * frame_dev + frame
                    dest[at_lane, pl.ds(place, cols, stride=row_dev * frames), :] = stage[
                        slot, pl.ds(start, cols, stride=unit), :
                    ]


def share_kernel(dims, halos, own, *refs):
    time_devs, row_devs, frame_dev, row_dev, col_dev = dims
    wins = refs[:time_devs]
    me = lax.axis_index("rows")
    targets = [me] if own else [to(me) for _, to, _ in pairing(row_devs)]
    outs = refs[time_devs : time_devs + len(targets)]
    scratch = refs[time_devs + len(targets) :]
    unit = frame_dev * row_dev
    ends = window_rows(halos, unit, row_devs * col_dev)
    sizes = window_rows(halos, row_dev * time_devs * frame_dev, col_dev)
    for at, target in enumerate(targets):
        for k, halo in enumerate(halos):
            stage, dest = scratch[2 * k], scratch[2 * k + 1]
            laid_out(dims, wins, halo, ends[k], target, stage, dest)
            for at_lane, lane in lanes(outs[at].shape[1]):
                value = dest[at_lane]
                if outs[at].dtype == F32:
                    value = silu_slope(value)
                outs[at][sizes[k] : sizes[k + 1], lane] = value.astype(outs[at].dtype)


def share(dims, halos, own, slopes, windows):
    time_devs, row_devs, frame_dev, row_dev, col_dev = dims
    channels = windows[0].shape[1]
    parts, unit, tall = channels // LANES, frame_dev * row_dev, row_dev * time_devs * frame_dev
    size = window_rows(halos, tall, col_dev)[-1]
    count = 1 if own else row_devs - 1
    scratch = []
    for halo in halos:
        rows = (row_devs * col_dev + 2 * halo) * unit
        scratch.append(pltpu.VMEM((time_devs * parts, rows, LANES), F32))
        scratch.append(pltpu.VMEM((parts, (col_dev + 2 * halo) * tall, LANES), F32))
    shape = jax.ShapeDtypeStruct((size, channels), F32 if slopes else BF16)
    return kernel_call(
        functools.partial(share_kernel, dims, halos, own),
        [shape] * count,
        [VMEM] * time_devs,
        scratch,
        10**8,
    )(*windows)


def row_sources(row_devs):
    me = lax.axis_index("rows")
    return [me] + [source(me) for _, _, source in pairing(row_devs)]


def spread(full, targets, cols, rows, frames):
    size = cols * (rows + 2) * frames
    place = lax.rem(lax.broadcasted_iota(jnp.int32, (size, LANES), 0), frames)
    for a, target in enumerate(targets):
        for p in range(2):
            count = size - p * frames
            for at_lane, lane in lanes(target.shape[2]):
                value = full[at_lane, pl.ds(a + p * frames, count), :]
                value = jnp.where(place[:count] < frames - a, value, 0.0).astype(BF16)
                target[p, 0:count, lane] = value


def tap(shifts, r, c, cols, rows, frames):
    parity = r % 2
    start = (r - parity) * frames
    pitch = (rows + 2) * frames
    return jnp.concatenate(
        [
            shifts[parity, (c + w) * pitch + start : (c + w) * pitch + start + rows * frames, :]
            for w in range(cols)
        ],
        axis=0,
    )


def taps_of(shifts, weights, cols, rows, frames):
    order = [(r, c) for r in range(3) for c in range(3)]
    moved = jnp.concatenate([tap(shifts, r, c, cols, rows, frames) for r, c in order], axis=1)
    mixed = jnp.concatenate([weights[2 - r, 2 - c] for r, c in order], axis=1)
    return moved, mixed


def first_kernel(dims, *refs):
    time_devs, row_devs, frame_dev, row_dev, col_dev = dims
    pieces, weight_ref = refs[:row_devs], refs[row_devs]
    acc_ref, mid_ref, full, shifts = refs[row_devs + 1 :]
    frames, rows = time_devs * frame_dev, row_devs * row_dev
    plane, pitch, tall = rows * frames, (rows + 2) * frames, row_dev * frames
    for w in range(col_dev + 4):
        edge = jnp.zeros((full.shape[0], frames, LANES), F32)
        full[:, w * pitch : w * pitch + frames, :] = edge
        full[:, (w + 1) * pitch - frames : (w + 1) * pitch, :] = edge
        for at, source in enumerate(row_sources(row_devs)):
            start = pl.multiple_of(w * pitch + frames + source * tall, frames)
            for at_lane, lane in lanes(acc_ref.shape[1]):
                full[at_lane, pl.ds(start, tall), :] = pieces[at][
                    w * tall : (w + 1) * tall, lane
                ].astype(F32)
    full[:, (col_dev + 4) * pitch :, :] = jnp.zeros((full.shape[0], frames, LANES), F32)
    spread(full, [shifts.at[a] for a in range(3)], col_dev + 4, rows, frames)
    for w in range(col_dev):
        start = (w + 2) * pitch + frames
        mid_ref[:, w * plane : (w + 1) * plane, :] = full[:, start : start + plane, :]
    acc_ref[...] = jnp.zeros_like(acc_ref)

    @pl.loop(0, 3)
    def _(a):
        moved, mixed = taps_of(shifts.at[a], weight_ref.at[2 - a], col_dev + 2, rows, frames)
        acc_ref[...] += dot_last(moved, mixed)


def second_kernel(dims, cols_all, *refs):
    time_devs, row_devs, frame_dev, row_dev, col_dev = dims
    pieces, acc_ref, mid_ref, weight_ref, out_ref = refs[:row_devs], *refs[row_devs : row_devs + 4]
    slopes, full, shifts, grad = refs[row_devs + 4 :]
    frames, rows = time_devs * frame_dev, row_devs * row_dev
    plane, pitch, tall = rows * frames, (rows + 2) * frames, row_dev * frames
    sizes = window_rows((1, 0), tall, col_dev)
    sources = row_sources(row_devs)
    first_col = (lax.axis_index("tm") * row_devs + lax.axis_index("rows")) * col_dev - 1

    def slope(at, begin, lane):
        value = pieces[at][begin : begin + tall, lane]
        return value if at == 0 else silu_slope(value.astype(F32))

    for w in range(col_dev + 2):
        col = first_col + w
        inside = jnp.logical_and(col >= 0, col < cols_all)
        edge = jnp.zeros((full.shape[0], frames, LANES), F32)
        full[:, w * pitch : w * pitch + frames, :] = edge
        full[:, (w + 1) * pitch - frames : (w + 1) * pitch, :] = edge
        for at, source in enumerate(sources):
            here = pl.multiple_of(w * plane + source * tall, frames)
            start = pl.multiple_of(w * pitch + frames + source * tall, frames)
            for at_lane, lane in lanes(acc_ref.shape[1]):
                value = acc_ref[pl.ds(here, tall), lane] * slope(at, w * tall, lane)
                full[at_lane, pl.ds(start, tall), :] = jnp.where(inside, value, 0.0)
    full[:, (col_dev + 2) * pitch :, :] = jnp.zeros((full.shape[0], frames, LANES), F32)
    spread(full, [shifts.at[a] for a in range(3)], col_dev + 2, rows, frames)
    grad[...] = jnp.zeros_like(grad)

    @pl.loop(0, 3)
    def _(a):
        moved, mixed = taps_of(shifts.at[a], weight_ref.at[2 - a], col_dev, rows, frames)
        grad[...] += dot_last(mixed, moved)

    for w in range(col_dev):
        for at, source in enumerate(sources):
            here = pl.multiple_of(w * plane + source * tall, frames)
            for at_lane, lane in lanes(acc_ref.shape[1]):
                slopes[at_lane, pl.ds(here, tall), :] = slope(at, sizes[1] + w * tall, lane)
    size = col_dev * plane
    for at_lane, lane in lanes(grad.shape[0]):
        full[at_lane, 0:size, :] = mid_ref[at_lane] + grad[lane, :].T * slopes[at_lane]
        for frame in range(frames):
            for row in range(rows):
                out_ref[0, frame, row, :, lane] = full[
                    at_lane, pl.ds(row * frames + frame, col_dev, stride=plane), :
                ]


def kernel_call(body, out_shape, in_specs, scratch, flops, room=24):
    return pl.pallas_call(
        body,
        out_shape=out_shape,
        in_specs=in_specs,
        out_specs=jax.tree.map(lambda _: VMEM, out_shape),
        scratch_shapes=scratch,
        compiler_params=pltpu.CompilerParams(vmem_limit_bytes=room << 20),
        cost_estimate=pl.CostEstimate(flops=flops, bytes_accessed=4 << 20, transcendentals=0),
    )


def on_device(latents, hidden, cotangent, conv_one, conv_two, lengths):
    _, frame_dev, row_dev, cols, channels = latents.shape
    time_devs, row_devs = lax.axis_size("tm"), lax.axis_size("rows")
    col_dev = cols // (time_devs * row_devs)
    frames, rows = time_devs * frame_dev, row_devs * row_dev
    dims = (time_devs, row_devs, frame_dev, row_dev, col_dev)
    plane, pitch = rows * frames, (rows + 2) * frames
    parts = channels // LANES

    def over_tm(windows):
        out = [windows[0]]
        for step, (pairs, _, _) in enumerate(pairing(time_devs)):
            out.append(lax.ppermute(windows[step + 1], "tm", pairs))
        return out

    def over_rows(pieces):
        out = []
        for at, (pairs, _, _) in enumerate(pairing(row_devs)):
            out.append(lax.ppermute(pieces[at], "rows", pairs))
        return out

    def for_rows(windows, halos, slopes):
        sent = []
        if row_devs > 1:
            sent = share(dims, halos, False, False, windows)
        own = share(dims, halos, True, slopes, windows)
        return [*own, *over_rows(sent)]

    def part_rows(size):
        return pltpu.VMEM((parts, size, LANES), F32)

    mac = 2 * 9 * channels * channels
    wide, narrow = (col_dev + 2) * plane, col_dev * plane
    cot = pack([cotangent[0]], lengths, (2,), True, time_devs)
    cot = for_rows(over_tm(cot), (2,), False)
    hid = pack([hidden[0], latents[0]], lengths, (1, 0), False, time_devs)
    hid = for_rows(over_tm(hid), (1, 0), True)
    acc, mid = kernel_call(
        functools.partial(first_kernel, dims),
        [
            jax.ShapeDtypeStruct((wide, channels), F32),
            jax.ShapeDtypeStruct((parts, narrow, LANES), F32),
        ],
        [VMEM] * (row_devs + 1),
        [
            part_rows((col_dev + 4) * pitch + frames),
            pltpu.VMEM((3, 2, (col_dev + 4) * pitch, channels), BF16),
        ],
        3 * mac * wide,
    )(*cot, conv_two)
    return kernel_call(
        functools.partial(second_kernel, dims, cols),
        jax.ShapeDtypeStruct((1, frames, rows, col_dev, channels), F32),
        [VMEM] * (row_devs + 3),
        [
            part_rows(narrow),
            part_rows((col_dev + 2) * pitch + frames),
            pltpu.VMEM((3, 2, (col_dev + 2) * pitch, channels), BF16),
            pltpu.VMEM((channels, narrow), F32),
        ],
        3 * mac * narrow,
    )(*hid, acc, mid, conv_one)


def solution(mesh):
    spec = P("dp", "tm", "rows", None, None)
    return jax.shard_map(
        on_device,
        mesh=mesh,
        in_specs=(spec, spec, spec, P(), P(), P("dp")),
        out_specs=P("dp", None, None, ("tm", "rows"), None),
        check_vma=False,
    )
```

```python
import functools

import jax
import jax.numpy as jnp
from jax import lax
from jax.experimental import pallas as pl
from jax.experimental.pallas import tpu as pltpu
from jax.sharding import PartitionSpec as P


F32 = jnp.float32
BF16 = jnp.bfloat16
VMEM = pl.BlockSpec(memory_space=pltpu.VMEM)
SMEM = pl.BlockSpec(memory_space=pltpu.SMEM)
LANES = 128
EARLY, LATE = (0,), (1, 2)
STEPS = {4: (3, 2, 1)}


def lanes(channels):
    return [(at, slice(at * LANES, (at + 1) * LANES)) for at in range(channels // LANES)]


def pairing(count):
    if count & (count - 1) == 0:
        return [
            ([(i, i ^ s) for i in range(count)], lambda i, s=s: i ^ s, lambda i, s=s: i ^ s)
            for s in STEPS.get(count, range(1, count))
        ]
    return [
        (
            [(i, (i + s) % count) for i in range(count)],
            lambda i, s=s: lax.rem(i + s, count),
            lambda i, s=s: lax.rem(i + count - s, count),
        )
        for s in range(1, count)
    ]


def silu_slope(values):
    sigmoid_of = jax.nn.sigmoid(values)
    return sigmoid_of * (1.0 + values * (1.0 - sigmoid_of))


def dot_last(a, b):
    return lax.dot_general(a, b, (((1,), (1,)), ((), ())), preferred_element_type=F32)


def window_rows(halos, unit, block):
    ends = [0]
    for halo in halos:
        ends.append(ends[-1] + (block + 2 * halo) * unit)
    return ends


def pack_kernel(time_devs, halos, masked, *refs):
    count = len(halos)
    len_ref, ins = refs[0], refs[1 : 1 + count]
    outs, turned = refs[1 + count : -count], refs[-count:]
    me = lax.axis_index("tm")
    targets = [me] + [to(me) for _, to, _ in pairing(time_devs)]
    frames, rows, cols, channels = ins[0].shape
    unit, block = frames * rows, cols // time_devs
    ends = window_rows(halos, unit, block)
    for at in range(count):
        ref, stage, halo = ins[at], turned[at], halos[at]
        if halo:
            edge = jnp.zeros((stage.shape[0], halo * unit, LANES), F32)
            stage[:, 0 : halo * unit, :] = edge
            stage[:, (halo + cols) * unit :, :] = edge
        for frame in range(frames):
            for row in range(rows):
                value = ref[frame, row].astype(F32)
                if masked:
                    value = jnp.where(me * frames + frame < len_ref[0], value, 0.0)
                start = halo * unit + frame * rows + row
                for at_lane, lane in lanes(channels):
                    stage[at_lane, pl.ds(start, cols, stride=unit), :] = value[:, lane]
        size = ends[at + 1] - ends[at]
        for step, target in enumerate(targets):
            start = pl.multiple_of(target * (block * unit), unit)
            for at_lane, lane in lanes(channels):
                outs[step][ends[at] : ends[at + 1], lane] = stage[
                    at_lane, pl.ds(start, size), :
                ].astype(BF16)


def pack(arrays, lengths, halos, masked, time_devs):
    frames, rows, cols, channels = arrays[0].shape
    unit = frames * rows
    size = window_rows(halos, unit, cols // time_devs)[-1]
    return pl.pallas_call(
        functools.partial(pack_kernel, time_devs, halos, masked),
        out_shape=[jax.ShapeDtypeStruct((size, channels), BF16)] * time_devs,
        in_specs=[SMEM] + [VMEM] * len(arrays),
        out_specs=[VMEM] * time_devs,
        scratch_shapes=[
            pltpu.VMEM((channels // LANES, (cols + 2 * halo) * unit, LANES), F32) for halo in halos
        ],
        compiler_params=pltpu.CompilerParams(vmem_limit_bytes=12 << 20),
        cost_estimate=pl.CostEstimate(
            flops=6 * 10**9, bytes_accessed=2 << 20, transcendentals=0
        ),
    )(lengths, *arrays)


def laid_out(dims, wins, halo, begin, target, stage, dest):
    time_devs, _, frame_dev, row_dev, col_dev = dims
    frames, unit = time_devs * frame_dev, frame_dev * row_dev
    tm = lax.axis_index("tm")
    from_tm = [tm] + [source(tm) for _, _, source in pairing(time_devs)]
    cols = col_dev + 2 * halo
    first = pl.multiple_of(target * (col_dev * unit), unit)
    for s in range(time_devs):
        for at_lane, lane in lanes(wins[s].shape[1]):
            slot = s * stage.shape[0] // time_devs + at_lane
            stage[slot] = wins[s][begin : begin + stage.shape[1], lane].astype(F32)
            for frame in range(frame_dev):
                for row in range(row_dev):
                    start = first + frame * row_dev + row
                    place = row * frames + from_tm[s] * frame_dev + frame
                    dest[at_lane, pl.ds(place, cols, stride=row_dev * frames), :] = stage[
                        slot, pl.ds(start, cols, stride=unit), :
                    ]


def share_kernel(dims, halos, own, *refs):
    time_devs, row_devs, frame_dev, row_dev, col_dev = dims
    wins = refs[:time_devs]
    me = lax.axis_index("rows")
    targets = [me] if own else [to(me) for _, to, _ in pairing(row_devs)]
    outs = refs[time_devs : time_devs + len(targets)]
    scratch = refs[time_devs + len(targets) :]
    unit = frame_dev * row_dev
    ends = window_rows(halos, unit, row_devs * col_dev)
    sizes = window_rows(halos, row_dev * time_devs * frame_dev, col_dev)
    for at, target in enumerate(targets):
        for k, halo in enumerate(halos):
            stage, dest = scratch[2 * k], scratch[2 * k + 1]
            laid_out(dims, wins, halo, ends[k], target, stage, dest)
            for at_lane, lane in lanes(outs[at].shape[1]):
                value = dest[at_lane]
                if outs[at].dtype == F32:
                    value = silu_slope(value)
                outs[at][sizes[k] : sizes[k + 1], lane] = value.astype(outs[at].dtype)


def share(dims, halos, own, slopes, windows):
    time_devs, row_devs, frame_dev, row_dev, col_dev = dims
    channels = windows[0].shape[1]
    parts, unit, tall = channels // LANES, frame_dev * row_dev, row_dev * time_devs * frame_dev
    size = window_rows(halos, tall, col_dev)[-1]
    count = 1 if own else row_devs - 1
    scratch = []
    for halo in halos:
        rows = (row_devs * col_dev + 2 * halo) * unit
        scratch.append(pltpu.VMEM((time_devs * parts, rows, LANES), F32))
        scratch.append(pltpu.VMEM((parts, (col_dev + 2 * halo) * tall, LANES), F32))
    shape = jax.ShapeDtypeStruct((size, channels), F32 if slopes else BF16)
    return kernel_call(
        functools.partial(share_kernel, dims, halos, own),
        [shape] * count,
        [VMEM] * time_devs,
        scratch,
        10**8,
    )(*windows)


def row_sources(row_devs):
    me = lax.axis_index("rows")
    return [me] + [source(me) for _, _, source in pairing(row_devs)]


def spread(full, targets, cols, rows, frames):
    size = cols * (rows + 2) * frames
    place = lax.rem(lax.broadcasted_iota(jnp.int32, (size, LANES), 0), frames)
    for a, target in enumerate(targets):
        for p in range(2):
            count = size - p * frames
            for at_lane, lane in lanes(target.shape[2]):
                value = full[at_lane, pl.ds(a + p * frames, count), :]
                if a:
                    value = jnp.where(place[:count] < frames - a, value, 0.0)
                target[p, 0:count, lane] = value.astype(BF16)


def tap(shifts, r, c, cols, rows, frames):
    parity = r % 2
    start = (r - parity) * frames
    pitch = (rows + 2) * frames
    return jnp.concatenate(
        [
            shifts[parity, (c + w) * pitch + start : (c + w) * pitch + start + rows * frames, :]
            for w in range(cols)
        ],
        axis=0,
    )


def taps_of(shifts, weights, cols, rows, frames, row_taps=(0, 1, 2)):
    order = [(r, c) for r in row_taps for c in range(3)]
    moved = jnp.concatenate([tap(shifts, r, c, cols, rows, frames) for r, c in order], axis=1)
    mixed = jnp.concatenate([weights[2 - r, 2 - c] for r, c in order], axis=1)
    return moved, mixed


def first_kernel(dims, *refs):
    time_devs, row_devs, frame_dev, row_dev, col_dev = dims
    pieces, weight_ref = refs[:row_devs], refs[row_devs]
    acc_ref, mid_ref, last_ref, full, shifts = refs[row_devs + 1 :]
    frames, rows = time_devs * frame_dev, row_devs * row_dev
    plane, pitch, tall = rows * frames, (rows + 2) * frames, row_dev * frames
    for w in range(col_dev + 4):
        edge = jnp.zeros((full.shape[0], frames, LANES), F32)
        full[:, w * pitch : w * pitch + frames, :] = edge
        full[:, (w + 1) * pitch - frames : (w + 1) * pitch, :] = edge
        for at, source in enumerate(row_sources(row_devs)):
            start = pl.multiple_of(w * pitch + frames + source * tall, frames)
            for at_lane, lane in lanes(acc_ref.shape[1]):
                full[at_lane, pl.ds(start, tall), :] = pieces[at][
                    w * tall : (w + 1) * tall, lane
                ].astype(F32)
    full[:, (col_dev + 4) * pitch :, :] = jnp.zeros((full.shape[0], frames, LANES), F32)
    spread(full, [shifts.at[0], shifts.at[1], last_ref], col_dev + 4, rows, frames)
    for w in range(col_dev):
        start = (w + 2) * pitch + frames
        mid_ref[:, w * plane : (w + 1) * plane, :] = full[:, start : start + plane, :]
    acc_ref[...] = jnp.zeros_like(acc_ref)

    @pl.loop(0, 2)
    def _(a):
        moved, mixed = taps_of(shifts.at[a], weight_ref.at[2 - a], col_dev + 2, rows, frames)
        acc_ref[...] += dot_last(moved, mixed)

    moved, mixed = taps_of(last_ref, weight_ref.at[0], col_dev + 2, rows, frames, EARLY)
    acc_ref[...] += dot_last(moved, mixed)


def last_tap_kernel(dims, cols, acc_in, shifts, weight_ref, acc_ref):
    time_devs, row_devs, frame_dev, row_dev, _ = dims
    frames, rows = time_devs * frame_dev, row_devs * row_dev
    moved, mixed = taps_of(shifts, weight_ref.at[0], cols, rows, frames, LATE)
    acc_ref[...] = acc_in[...] + dot_last(moved, mixed)


def second_kernel(dims, cols_all, *refs):
    time_devs, row_devs, frame_dev, row_dev, col_dev = dims
    pieces, acc_ref, mid_ref, weight_ref, out_ref = refs[:row_devs], *refs[row_devs : row_devs + 4]
    slopes, full, shifts, grad = refs[row_devs + 4 :]
    frames, rows = time_devs * frame_dev, row_devs * row_dev
    plane, pitch, tall = rows * frames, (rows + 2) * frames, row_dev * frames
    sizes = window_rows((1, 0), tall, col_dev)
    sources = row_sources(row_devs)
    first_col = (lax.axis_index("tm") * row_devs + lax.axis_index("rows")) * col_dev - 1

    def slope(at, begin, lane):
        value = pieces[at][begin : begin + tall, lane]
        return value if at == 0 else silu_slope(value.astype(F32))

    for w in range(col_dev + 2):
        col = first_col + w
        inside = jnp.logical_and(col >= 0, col < cols_all)
        edge = jnp.zeros((full.shape[0], frames, LANES), F32)
        full[:, w * pitch : w * pitch + frames, :] = edge
        full[:, (w + 1) * pitch - frames : (w + 1) * pitch, :] = edge
        for at, source in enumerate(sources):
            here = pl.multiple_of(w * plane + source * tall, frames)
            start = pl.multiple_of(w * pitch + frames + source * tall, frames)
            for at_lane, lane in lanes(acc_ref.shape[1]):
                value = acc_ref[pl.ds(here, tall), lane] * slope(at, w * tall, lane)
                full[at_lane, pl.ds(start, tall), :] = jnp.where(inside, value, 0.0)
    full[:, (col_dev + 2) * pitch :, :] = jnp.zeros((full.shape[0], frames, LANES), F32)
    spread(full, [shifts.at[a] for a in range(3)], col_dev + 2, rows, frames)
    grad[...] = jnp.zeros_like(grad)

    @pl.loop(0, 3)
    def _(a):
        moved, mixed = taps_of(shifts.at[a], weight_ref.at[2 - a], col_dev, rows, frames)
        grad[...] += dot_last(mixed, moved)

    for w in range(col_dev):
        for at, source in enumerate(sources):
            here = pl.multiple_of(w * plane + source * tall, frames)
            for at_lane, lane in lanes(acc_ref.shape[1]):
                slopes[at_lane, pl.ds(here, tall), :] = slope(at, sizes[1] + w * tall, lane)
    size = col_dev * plane
    for at_lane, lane in lanes(grad.shape[0]):
        full[at_lane, 0:size, :] = mid_ref[at_lane] + grad[lane, :].T * slopes[at_lane]
        for frame in range(frames):
            for row in range(rows):
                out_ref[0, frame, row, :, lane] = full[
                    at_lane, pl.ds(row * frames + frame, col_dev, stride=plane), :
                ]


def kernel_call(body, out_shape, in_specs, scratch, flops, room=24):
    return pl.pallas_call(
        body,
        out_shape=out_shape,
        in_specs=in_specs,
        out_specs=jax.tree.map(lambda _: VMEM, out_shape),
        scratch_shapes=scratch,
        compiler_params=pltpu.CompilerParams(vmem_limit_bytes=room << 20),
        cost_estimate=pl.CostEstimate(flops=flops, bytes_accessed=4 << 20, transcendentals=0),
    )


def on_device(latents, hidden, cotangent, conv_one, conv_two, lengths):
    _, frame_dev, row_dev, cols, channels = latents.shape
    time_devs, row_devs = lax.axis_size("tm"), lax.axis_size("rows")
    col_dev = cols // (time_devs * row_devs)
    frames, rows = time_devs * frame_dev, row_devs * row_dev
    dims = (time_devs, row_devs, frame_dev, row_dev, col_dev)
    plane, pitch = rows * frames, (rows + 2) * frames
    parts = channels // LANES

    def over_tm(windows):
        out = [windows[0]]
        for step, (pairs, _, _) in enumerate(pairing(time_devs)):
            out.append(lax.ppermute(windows[step + 1], "tm", pairs))
        return out

    def over_rows(pieces):
        out = []
        for at, (pairs, _, _) in enumerate(pairing(row_devs)):
            out.append(lax.ppermute(pieces[at], "rows", pairs))
        return out

    def for_rows(windows, halos, slopes):
        sent = []
        if row_devs > 1:
            sent = share(dims, halos, False, False, windows)
        own = share(dims, halos, True, slopes, windows)
        return [*own, *over_rows(sent)]

    def part_rows(size):
        return pltpu.VMEM((parts, size, LANES), F32)

    mac = 2 * 9 * channels * channels
    wide, narrow = (col_dev + 2) * plane, col_dev * plane
    cot = pack([cotangent[0]], lengths, (2,), True, time_devs)
    cot = for_rows(over_tm(cot), (2,), False)
    hid = pack([hidden[0], latents[0]], lengths, (1, 0), False, time_devs)
    hid = for_rows(over_tm(hid), (1, 0), True)
    acc, mid, moved = kernel_call(
        functools.partial(first_kernel, dims),
        [
            jax.ShapeDtypeStruct((wide, channels), F32),
            jax.ShapeDtypeStruct((parts, narrow, LANES), F32),
            jax.ShapeDtypeStruct((2, (col_dev + 4) * pitch, channels), BF16),
        ],
        [VMEM] * (row_devs + 1),
        [
            part_rows((col_dev + 4) * pitch + frames),
            pltpu.VMEM((2, 2, (col_dev + 4) * pitch, channels), BF16),
        ],
        3 * mac * wide,
    )(*cot, conv_two)
    acc = kernel_call(
        functools.partial(last_tap_kernel, dims, col_dev + 2),
        jax.ShapeDtypeStruct((wide, channels), F32),
        [VMEM] * 3,
        [],
        mac * wide,
    )(acc, moved, conv_two)
    return kernel_call(
        functools.partial(second_kernel, dims, cols),
        jax.ShapeDtypeStruct((1, frames, rows, col_dev, channels), F32),
        [VMEM] * (row_devs + 3),
        [
            part_rows(narrow),
            part_rows((col_dev + 2) * pitch + frames),
            pltpu.VMEM((3, 2, (col_dev + 2) * pitch, channels), BF16),
            pltpu.VMEM((channels, narrow), F32),
        ],
        3 * mac * narrow,
    )(*hid, acc, mid, conv_one)


def solution(mesh):
    spec = P("dp", "tm", "rows", None, None)
    return jax.shard_map(
        on_device,
        mesh=mesh,
        in_specs=(spec, spec, spec, P(), P(), P("dp")),
        out_specs=P("dp", None, None, ("tm", "rows"), None),
        check_vma=False,
    )
```

```python
import functools

import jax
import jax.numpy as jnp
from jax import lax
from jax.experimental import pallas as pl
from jax.experimental.pallas import tpu as pltpu
from jax.sharding import PartitionSpec as P


F32 = jnp.float32
BF16 = jnp.bfloat16
VMEM = pl.BlockSpec(memory_space=pltpu.VMEM)
SMEM = pl.BlockSpec(memory_space=pltpu.SMEM)
LANES = 128
EARLY, LATE = (0, 1), (2,)
STEPS = {4: (3, 2, 1)}


def lanes(channels):
    return [(at, slice(at * LANES, (at + 1) * LANES)) for at in range(channels // LANES)]


def pairing(count):
    if count & (count - 1) == 0:
        return [
            ([(i, i ^ s) for i in range(count)], lambda i, s=s: i ^ s, lambda i, s=s: i ^ s)
            for s in STEPS.get(count, range(1, count))
        ]
    return [
        (
            [(i, (i + s) % count) for i in range(count)],
            lambda i, s=s: lax.rem(i + s, count),
            lambda i, s=s: lax.rem(i + count - s, count),
        )
        for s in range(1, count)
    ]


def silu_slope(values):
    sigmoid_of = jax.nn.sigmoid(values)
    return sigmoid_of * (1.0 + values * (1.0 - sigmoid_of))


def dot_last(a, b):
    return lax.dot_general(a, b, (((1,), (1,)), ((), ())), preferred_element_type=F32)


def window_rows(halos, unit, block):
    ends = [0]
    for halo in halos:
        ends.append(ends[-1] + (block + 2 * halo) * unit)
    return ends


def pack_kernel(time_devs, halos, masked, *refs):
    count = len(halos)
    len_ref, ins = refs[0], refs[1 : 1 + count]
    outs, turned = refs[1 + count : -count], refs[-count:]
    me = lax.axis_index("tm")
    targets = [me] + [to(me) for _, to, _ in pairing(time_devs)]
    frames, rows, cols, channels = ins[0].shape
    unit, block = frames * rows, cols // time_devs
    ends = window_rows(halos, unit, block)
    for at in range(count):
        ref, stage, halo = ins[at], turned[at], halos[at]
        if halo:
            edge = jnp.zeros((stage.shape[0], halo * unit, LANES), F32)
            stage[:, 0 : halo * unit, :] = edge
            stage[:, (halo + cols) * unit :, :] = edge
        for frame in range(frames):
            for row in range(rows):
                value = ref[frame, row].astype(F32)
                if masked:
                    value = jnp.where(me * frames + frame < len_ref[0], value, 0.0)
                start = halo * unit + frame * rows + row
                for at_lane, lane in lanes(channels):
                    stage[at_lane, pl.ds(start, cols, stride=unit), :] = value[:, lane]
        size = ends[at + 1] - ends[at]
        for step, target in enumerate(targets):
            start = pl.multiple_of(target * (block * unit), unit)
            for at_lane, lane in lanes(channels):
                outs[step][ends[at] : ends[at + 1], lane] = stage[
                    at_lane, pl.ds(start, size), :
                ].astype(BF16)


def pack(arrays, lengths, halos, masked, time_devs):
    frames, rows, cols, channels = arrays[0].shape
    unit = frames * rows
    size = window_rows(halos, unit, cols // time_devs)[-1]
    return pl.pallas_call(
        functools.partial(pack_kernel, time_devs, halos, masked),
        out_shape=[jax.ShapeDtypeStruct((size, channels), BF16)] * time_devs,
        in_specs=[SMEM] + [VMEM] * len(arrays),
        out_specs=[VMEM] * time_devs,
        scratch_shapes=[
            pltpu.VMEM((channels // LANES, (cols + 2 * halo) * unit, LANES), F32) for halo in halos
        ],
        compiler_params=pltpu.CompilerParams(vmem_limit_bytes=12 << 20),
        cost_estimate=pl.CostEstimate(
            flops=6 * 10**9, bytes_accessed=2 << 20, transcendentals=0
        ),
    )(lengths, *arrays)


def laid_out(dims, wins, halo, begin, target, stage, dest):
    time_devs, _, frame_dev, row_dev, col_dev = dims
    frames, unit = time_devs * frame_dev, frame_dev * row_dev
    tm = lax.axis_index("tm")
    from_tm = [tm] + [source(tm) for _, _, source in pairing(time_devs)]
    cols = col_dev + 2 * halo
    first = pl.multiple_of(target * (col_dev * unit), unit)
    for s in range(time_devs):
        for at_lane, lane in lanes(wins[s].shape[1]):
            slot = s * stage.shape[0] // time_devs + at_lane
            stage[slot] = wins[s][begin : begin + stage.shape[1], lane].astype(F32)
            for frame in range(frame_dev):
                for row in range(row_dev):
                    start = first + frame * row_dev + row
                    place = row * frames + from_tm[s] * frame_dev + frame
                    dest[at_lane, pl.ds(place, cols, stride=row_dev * frames), :] = stage[
                        slot, pl.ds(start, cols, stride=unit), :
                    ]


def share_kernel(dims, halos, own, *refs):
    time_devs, row_devs, frame_dev, row_dev, col_dev = dims
    wins = refs[:time_devs]
    me = lax.axis_index("rows")
    targets = [me] if own else [to(me) for _, to, _ in pairing(row_devs)]
    outs = refs[time_devs : time_devs + len(targets)]
    scratch = refs[time_devs + len(targets) :]
    unit = frame_dev * row_dev
    ends = window_rows(halos, unit, row_devs * col_dev)
    sizes = window_rows(halos, row_dev * time_devs * frame_dev, col_dev)
    for at, target in enumerate(targets):
        for k, halo in enumerate(halos):
            stage, dest = scratch[2 * k], scratch[2 * k + 1]
            laid_out(dims, wins, halo, ends[k], target, stage, dest)
            for at_lane, lane in lanes(outs[at].shape[1]):
                value = dest[at_lane]
                if outs[at].dtype == F32:
                    value = silu_slope(value)
                outs[at][sizes[k] : sizes[k + 1], lane] = value.astype(outs[at].dtype)


def share(dims, halos, own, slopes, windows):
    time_devs, row_devs, frame_dev, row_dev, col_dev = dims
    channels = windows[0].shape[1]
    parts, unit, tall = channels // LANES, frame_dev * row_dev, row_dev * time_devs * frame_dev
    size = window_rows(halos, tall, col_dev)[-1]
    count = 1 if own else row_devs - 1
    scratch = []
    for halo in halos:
        rows = (row_devs * col_dev + 2 * halo) * unit
        scratch.append(pltpu.VMEM((time_devs * parts, rows, LANES), F32))
        scratch.append(pltpu.VMEM((parts, (col_dev + 2 * halo) * tall, LANES), F32))
    shape = jax.ShapeDtypeStruct((size, channels), F32 if slopes else BF16)
    return kernel_call(
        functools.partial(share_kernel, dims, halos, own),
        [shape] * count,
        [VMEM] * time_devs,
        scratch,
        10**8,
    )(*windows)


def row_sources(row_devs):
    me = lax.axis_index("rows")
    return [me] + [source(me) for _, _, source in pairing(row_devs)]


def spread(full, target, a, cols, rows, frames):
    size = cols * (rows + 2) * frames
    place = lax.rem(lax.broadcasted_iota(jnp.int32, (size, LANES), 0), frames)
    for p in range(2):
        count = size - p * frames
        for at_lane, lane in lanes(target.shape[2]):
            value = full[at_lane, pl.ds(a + p * frames, count), :]
            if a:
                value = jnp.where(place[:count] < frames - a, value, 0.0)
            target[p, 0:count, lane] = value.astype(BF16)


def tap(shifts, r, c, cols, rows, frames):
    parity = r % 2
    start = (r - parity) * frames
    pitch = (rows + 2) * frames
    return jnp.concatenate(
        [
            shifts[parity, (c + w) * pitch + start : (c + w) * pitch + start + rows * frames, :]
            for w in range(cols)
        ],
        axis=0,
    )


def taps_of(shifts, weights, cols, rows, frames, row_taps=(0, 1, 2)):
    order = [(r, c) for r in row_taps for c in range(3)]
    moved = jnp.concatenate([tap(shifts, r, c, cols, rows, frames) for r, c in order], axis=1)
    mixed = jnp.concatenate([weights[2 - r, 2 - c] for r, c in order], axis=1)
    return moved, mixed


def first_kernel(dims, *refs):
    time_devs, row_devs, frame_dev, row_dev, col_dev = dims
    pieces, weight_ref = refs[:row_devs], refs[row_devs]
    acc_ref, mid_ref, last_ref, full, *shifts = refs[row_devs + 1 :]
    frames, rows = time_devs * frame_dev, row_devs * row_dev
    plane, pitch, tall = rows * frames, (rows + 2) * frames, row_dev * frames
    for w in range(col_dev + 4):
        edge = jnp.zeros((full.shape[0], frames, LANES), F32)
        full[:, w * pitch : w * pitch + frames, :] = edge
        full[:, (w + 1) * pitch - frames : (w + 1) * pitch, :] = edge
        for at, source in enumerate(row_sources(row_devs)):
            start = pl.multiple_of(w * pitch + frames + source * tall, frames)
            for at_lane, lane in lanes(acc_ref.shape[1]):
                full[at_lane, pl.ds(start, tall), :] = pieces[at][
                    w * tall : (w + 1) * tall, lane
                ].astype(F32)
    full[:, (col_dev + 4) * pitch :, :] = jnp.zeros((full.shape[0], frames, LANES), F32)
    for w in range(col_dev):
        start = (w + 2) * pitch + frames
        mid_ref[:, w * plane : (w + 1) * plane, :] = full[:, start : start + plane, :]
    shifts.append(last_ref)
    for a in range(3):
        spread(full, shifts[a], a, col_dev + 4, rows, frames)
        row_taps = (0, 1, 2) if a < 2 else EARLY
        moved, mixed = taps_of(
            shifts[a], weight_ref.at[2 - a], col_dev + 2, rows, frames, row_taps
        )
        part = dot_last(moved, mixed)
        acc_ref[...] = acc_ref[...] + part if a else part


def last_tap_kernel(dims, cols, acc_in, shifts, weight_ref, acc_ref):
    time_devs, row_devs, frame_dev, row_dev, _ = dims
    frames, rows = time_devs * frame_dev, row_devs * row_dev
    moved, mixed = taps_of(shifts, weight_ref.at[0], cols, rows, frames, LATE)
    acc_ref[...] = acc_in[...] + dot_last(moved, mixed)


def second_kernel(dims, cols_all, *refs):
    time_devs, row_devs, frame_dev, row_dev, col_dev = dims
    pieces, acc_ref, mid_ref, weight_ref, out_ref = refs[:row_devs], *refs[row_devs : row_devs + 4]
    slopes, full, grad, *shifts = refs[row_devs + 4 :]
    frames, rows = time_devs * frame_dev, row_devs * row_dev
    plane, pitch, tall = rows * frames, (rows + 2) * frames, row_dev * frames
    sizes = window_rows((1, 0), tall, col_dev)
    sources = row_sources(row_devs)
    first_col = (lax.axis_index("tm") * row_devs + lax.axis_index("rows")) * col_dev - 1

    def slope(at, begin, lane):
        value = pieces[at][begin : begin + tall, lane]
        return value if at == 0 else silu_slope(value.astype(F32))

    for w in range(col_dev + 2):
        col = first_col + w
        inside = jnp.logical_and(col >= 0, col < cols_all)
        edge = jnp.zeros((full.shape[0], frames, LANES), F32)
        full[:, w * pitch : w * pitch + frames, :] = edge
        full[:, (w + 1) * pitch - frames : (w + 1) * pitch, :] = edge
        for at, source in enumerate(sources):
            here = pl.multiple_of(w * plane + source * tall, frames)
            start = pl.multiple_of(w * pitch + frames + source * tall, frames)
            for at_lane, lane in lanes(acc_ref.shape[1]):
                value = acc_ref[pl.ds(here, tall), lane] * slope(at, w * tall, lane)
                full[at_lane, pl.ds(start, tall), :] = jnp.where(inside, value, 0.0)
    full[:, (col_dev + 2) * pitch :, :] = jnp.zeros((full.shape[0], frames, LANES), F32)
    for a in range(3):
        spread(full, shifts[a], a, col_dev + 2, rows, frames)
        moved, mixed = taps_of(shifts[a], weight_ref.at[2 - a], col_dev, rows, frames)
        part = dot_last(mixed, moved)
        grad[...] = grad[...] + part if a else part
    for w in range(col_dev):
        for at, source in enumerate(sources):
            here = pl.multiple_of(w * plane + source * tall, frames)
            for at_lane, lane in lanes(acc_ref.shape[1]):
                slopes[at_lane, pl.ds(here, tall), :] = slope(at, sizes[1] + w * tall, lane)
    size = col_dev * plane
    for at_lane, lane in lanes(grad.shape[0]):
        full[at_lane, 0:size, :] = mid_ref[at_lane] + grad[lane, :].T * slopes[at_lane]
        for frame in range(frames):
            for row in range(rows):
                out_ref[0, frame, row, :, lane] = full[
                    at_lane, pl.ds(row * frames + frame, col_dev, stride=plane), :
                ]


def kernel_call(body, out_shape, in_specs, scratch, flops, room=24):
    return pl.pallas_call(
        body,
        out_shape=out_shape,
        in_specs=in_specs,
        out_specs=jax.tree.map(lambda _: VMEM, out_shape),
        scratch_shapes=scratch,
        compiler_params=pltpu.CompilerParams(vmem_limit_bytes=room << 20),
        cost_estimate=pl.CostEstimate(flops=flops, bytes_accessed=4 << 20, transcendentals=0),
    )


def on_device(latents, hidden, cotangent, conv_one, conv_two, lengths):
    _, frame_dev, row_dev, cols, channels = latents.shape
    time_devs, row_devs = lax.axis_size("tm"), lax.axis_size("rows")
    col_dev = cols // (time_devs * row_devs)
    frames, rows = time_devs * frame_dev, row_devs * row_dev
    dims = (time_devs, row_devs, frame_dev, row_dev, col_dev)
    plane, pitch = rows * frames, (rows + 2) * frames
    parts = channels // LANES

    def over_tm(windows):
        out = [windows[0]]
        for step, (pairs, _, _) in enumerate(pairing(time_devs)):
            out.append(lax.ppermute(windows[step + 1], "tm", pairs))
        return out

    def over_rows(pieces):
        out = []
        for at, (pairs, _, _) in enumerate(pairing(row_devs)):
            out.append(lax.ppermute(pieces[at], "rows", pairs))
        return out

    def for_rows(windows, halos, slopes):
        sent = []
        if row_devs > 1:
            sent = share(dims, halos, False, False, windows)
        own = share(dims, halos, True, slopes, windows)
        return [*own, *over_rows(sent)]

    def part_rows(size):
        return pltpu.VMEM((parts, size, LANES), F32)

    mac = 2 * 9 * channels * channels
    wide, narrow = (col_dev + 2) * plane, col_dev * plane
    cot = pack([cotangent[0]], lengths, (2,), True, time_devs)
    cot = for_rows(over_tm(cot), (2,), False)
    hid = pack([hidden[0], latents[0]], lengths, (1, 0), False, time_devs)
    hid = for_rows(over_tm(hid), (1, 0), True)
    acc, mid, moved = kernel_call(
        functools.partial(first_kernel, dims),
        [
            jax.ShapeDtypeStruct((wide, channels), F32),
            jax.ShapeDtypeStruct((parts, narrow, LANES), F32),
            jax.ShapeDtypeStruct((2, (col_dev + 4) * pitch, channels), BF16),
        ],
        [VMEM] * (row_devs + 1),
        [
            part_rows((col_dev + 4) * pitch + frames),
            *[pltpu.VMEM((2, (col_dev + 4) * pitch, channels), BF16)] * 2,
        ],
        3 * mac * wide,
    )(*cot, conv_two)
    acc = kernel_call(
        functools.partial(last_tap_kernel, dims, col_dev + 2),
        jax.ShapeDtypeStruct((wide, channels), F32),
        [VMEM] * 3,
        [],
        mac * wide,
    )(acc, moved, conv_two)
    return kernel_call(
        functools.partial(second_kernel, dims, cols),
        jax.ShapeDtypeStruct((1, frames, rows, col_dev, channels), F32),
        [VMEM] * (row_devs + 3),
        [
            part_rows(narrow),
            part_rows((col_dev + 2) * pitch + frames),
            pltpu.VMEM((channels, narrow), F32),
            *[pltpu.VMEM((2, (col_dev + 2) * pitch, channels), BF16)] * 3,
        ],
        3 * mac * narrow,
    )(*hid, acc, mid, conv_one)


def solution(mesh):
    spec = P("dp", "tm", "rows", None, None)
    return jax.shard_map(
        on_device,
        mesh=mesh,
        in_specs=(spec, spec, spec, P(), P(), P("dp")),
        out_specs=P("dp", None, None, ("tm", "rows"), None),
        check_vma=False,
    )
```

```python
import functools

import jax
import jax.numpy as jnp
from jax import lax
from jax.experimental import pallas as pl
from jax.experimental.pallas import tpu as pltpu
from jax.sharding import PartitionSpec as P


F32 = jnp.float32
BF16 = jnp.bfloat16
VMEM = pl.BlockSpec(memory_space=pltpu.VMEM)
SMEM = pl.BlockSpec(memory_space=pltpu.SMEM)
LANES = 128
EARLY, LATE = (0, 1), (2,)
STEPS = {4: (3, 2, 1)}


def lanes(channels):
    return [(at, slice(at * LANES, (at + 1) * LANES)) for at in range(channels // LANES)]


def pairing(count):
    if count & (count - 1) == 0:
        return [
            ([(i, i ^ s) for i in range(count)], lambda i, s=s: i ^ s, lambda i, s=s: i ^ s)
            for s in STEPS.get(count, range(1, count))
        ]
    return [
        (
            [(i, (i + s) % count) for i in range(count)],
            lambda i, s=s: lax.rem(i + s, count),
            lambda i, s=s: lax.rem(i + count - s, count),
        )
        for s in range(1, count)
    ]


def silu_slope(values):
    sigmoid_of = jax.nn.sigmoid(values)
    return sigmoid_of * (1.0 + values * (1.0 - sigmoid_of))


def dot_last(a, b):
    return lax.dot_general(a, b, (((1,), (1,)), ((), ())), preferred_element_type=F32)


def window_rows(halos, unit, block):
    ends = [0]
    for halo in halos:
        ends.append(ends[-1] + (block + 2 * halo) * unit)
    return ends


def pack_kernel(time_devs, halos, masked, *refs):
    count = len(halos)
    len_ref, ins = refs[0], refs[1 : 1 + count]
    outs, turned = refs[1 + count : -count], refs[-count:]
    me = lax.axis_index("tm")
    targets = [me] + [to(me) for _, to, _ in pairing(time_devs)]
    frames, rows, cols, channels = ins[0].shape
    unit, block = frames * rows, cols // time_devs
    ends = window_rows(halos, unit, block)
    for at in range(count):
        ref, stage, halo = ins[at], turned[at], halos[at]
        if halo:
            edge = jnp.zeros((stage.shape[0], halo * unit, LANES), F32)
            stage[:, 0 : halo * unit, :] = edge
            stage[:, (halo + cols) * unit :, :] = edge
        for frame in range(frames):
            for row in range(rows):
                value = ref[frame, row].astype(F32)
                if masked:
                    value = jnp.where(me * frames + frame < len_ref[0], value, 0.0)
                start = halo * unit + frame * rows + row
                for at_lane, lane in lanes(channels):
                    stage[at_lane, pl.ds(start, cols, stride=unit), :] = value[:, lane]
        size = ends[at + 1] - ends[at]
        for step, target in enumerate(targets):
            start = pl.multiple_of(target * (block * unit), unit)
            for at_lane, lane in lanes(channels):
                outs[step][ends[at] : ends[at + 1], lane] = stage[
                    at_lane, pl.ds(start, size), :
                ].astype(BF16)


def pack(arrays, lengths, halos, masked, time_devs):
    frames, rows, cols, channels = arrays[0].shape
    unit = frames * rows
    size = window_rows(halos, unit, cols // time_devs)[-1]
    return pl.pallas_call(
        functools.partial(pack_kernel, time_devs, halos, masked),
        out_shape=[jax.ShapeDtypeStruct((size, channels), BF16)] * time_devs,
        in_specs=[SMEM] + [VMEM] * len(arrays),
        out_specs=[VMEM] * time_devs,
        scratch_shapes=[
            pltpu.VMEM((channels // LANES, (cols + 2 * halo) * unit, LANES), F32) for halo in halos
        ],
        compiler_params=pltpu.CompilerParams(vmem_limit_bytes=12 << 20),
        cost_estimate=pl.CostEstimate(
            flops=6 * 10**9, bytes_accessed=2 << 20, transcendentals=0
        ),
    )(lengths, *arrays)


def laid_out(dims, wins, halo, begin, target, stage, dest):
    time_devs, _, frame_dev, row_dev, col_dev = dims
    frames, unit = time_devs * frame_dev, frame_dev * row_dev
    tm = lax.axis_index("tm")
    from_tm = [tm] + [source(tm) for _, _, source in pairing(time_devs)]
    cols = col_dev + 2 * halo
    first = pl.multiple_of(target * (col_dev * unit), col_dev * unit)
    size = cols * unit
    narrow = (col_dev * unit) % 16 == 0 and begin % 16 == 0 and size % 16 == 0
    for s in range(time_devs):
        for at_lane, lane in lanes(wins[s].shape[1]):
            slot = s * stage.shape[0] // time_devs + at_lane
            if narrow:
                stage[slot, 0:size, :] = wins[s][pl.ds(begin + first, size), lane].astype(F32)
            else:
                stage[slot] = wins[s][begin : begin + stage.shape[1], lane].astype(F32)
            base = 0 if narrow else first
            for frame in range(frame_dev):
                for row in range(row_dev):
                    start = base + frame * row_dev + row
                    place = row * frames + from_tm[s] * frame_dev + frame
                    dest[at_lane, pl.ds(place, cols, stride=row_dev * frames), :] = stage[
                        slot, pl.ds(start, cols, stride=unit), :
                    ]


def share_kernel(dims, halos, own, *refs):
    time_devs, row_devs, frame_dev, row_dev, col_dev = dims
    wins = refs[:time_devs]
    me = lax.axis_index("rows")
    targets = [me] if own else [to(me) for _, to, _ in pairing(row_devs)]
    outs = refs[time_devs : time_devs + len(targets)]
    scratch = refs[time_devs + len(targets) :]
    unit = frame_dev * row_dev
    ends = window_rows(halos, unit, row_devs * col_dev)
    sizes = window_rows(halos, row_dev * time_devs * frame_dev, col_dev)
    for at, target in enumerate(targets):
        for k, halo in enumerate(halos):
            stage, dest = scratch[2 * k], scratch[2 * k + 1]
            laid_out(dims, wins, halo, ends[k], target, stage, dest)
            for at_lane, lane in lanes(outs[at].shape[1]):
                value = dest[at_lane]
                if outs[at].dtype == F32:
                    value = silu_slope(value)
                outs[at][sizes[k] : sizes[k + 1], lane] = value.astype(outs[at].dtype)


def share(dims, halos, own, slopes, windows):
    time_devs, row_devs, frame_dev, row_dev, col_dev = dims
    channels = windows[0].shape[1]
    parts, unit, tall = channels // LANES, frame_dev * row_dev, row_dev * time_devs * frame_dev
    size = window_rows(halos, tall, col_dev)[-1]
    count = 1 if own else row_devs - 1
    scratch = []
    for halo in halos:
        rows = (row_devs * col_dev + 2 * halo) * unit
        scratch.append(pltpu.VMEM((time_devs * parts, rows, LANES), F32))
        scratch.append(pltpu.VMEM((parts, (col_dev + 2 * halo) * tall, LANES), F32))
    shape = jax.ShapeDtypeStruct((size, channels), F32 if slopes else BF16)
    return kernel_call(
        functools.partial(share_kernel, dims, halos, own),
        [shape] * count,
        [VMEM] * time_devs,
        scratch,
        10**8,
    )(*windows)


def row_sources(row_devs):
    me = lax.axis_index("rows")
    return [me] + [source(me) for _, _, source in pairing(row_devs)]


def spread(full, target, a, cols, rows, frames):
    size = cols * (rows + 2) * frames
    place = lax.rem(lax.broadcasted_iota(jnp.int32, (size, LANES), 0), frames)
    for p in range(2):
        count = size - p * frames
        for at_lane, lane in lanes(target.shape[2]):
            value = full[at_lane, pl.ds(a + p * frames, count), :]
            if a:
                value = jnp.where(place[:count] < frames - a, value, 0.0)
            target[p, 0:count, lane] = value.astype(BF16)


def tap(shifts, r, c, cols, rows, frames):
    parity = r % 2
    start = (r - parity) * frames
    pitch = (rows + 2) * frames
    return jnp.concatenate(
        [
            shifts[parity, (c + w) * pitch + start : (c + w) * pitch + start + rows * frames, :]
            for w in range(cols)
        ],
        axis=0,
    )


def taps_of(shifts, weights, cols, rows, frames, row_taps=(0, 1, 2)):
    order = [(r, c) for r in row_taps for c in range(3)]
    moved = jnp.concatenate([tap(shifts, r, c, cols, rows, frames) for r, c in order], axis=1)
    mixed = jnp.concatenate([weights[2 - r, 2 - c] for r, c in order], axis=1)
    return moved, mixed


def first_kernel(dims, *refs):
    time_devs, row_devs, frame_dev, row_dev, col_dev = dims
    pieces, weight_ref = refs[:row_devs], refs[row_devs]
    acc_ref, mid_ref, last_ref, full, *shifts = refs[row_devs + 1 :]
    frames, rows = time_devs * frame_dev, row_devs * row_dev
    plane, pitch, tall = rows * frames, (rows + 2) * frames, row_dev * frames
    for w in range(col_dev + 4):
        edge = jnp.zeros((full.shape[0], frames, LANES), F32)
        full[:, w * pitch : w * pitch + frames, :] = edge
        full[:, (w + 1) * pitch - frames : (w + 1) * pitch, :] = edge
        for at, source in enumerate(row_sources(row_devs)):
            start = pl.multiple_of(w * pitch + frames + source * tall, frames)
            for at_lane, lane in lanes(acc_ref.shape[1]):
                full[at_lane, pl.ds(start, tall), :] = pieces[at][
                    w * tall : (w + 1) * tall, lane
                ].astype(F32)
    full[:, (col_dev + 4) * pitch :, :] = jnp.zeros((full.shape[0], frames, LANES), F32)
    for w in range(col_dev):
        start = (w + 2) * pitch + frames
        mid_ref[:, w * plane : (w + 1) * plane, :] = full[:, start : start + plane, :]
    shifts.append(last_ref)
    for a in range(3):
        spread(full, shifts[a], a, col_dev + 4, rows, frames)
        row_taps = (0, 1, 2) if a < 2 else EARLY
        moved, mixed = taps_of(
            shifts[a], weight_ref.at[2 - a], col_dev + 2, rows, frames, row_taps
        )
        part = dot_last(moved, mixed)
        acc_ref[...] = acc_ref[...] + part if a else part


def last_tap_kernel(dims, cols, acc_in, shifts, weight_ref, own_ref, acc_ref):
    time_devs, row_devs, frame_dev, row_dev, _ = dims
    frames, rows = time_devs * frame_dev, row_devs * row_dev
    moved, mixed = taps_of(shifts, weight_ref.at[0], cols, rows, frames, LATE)
    acc_ref[...] = acc_in[...] + dot_last(moved, mixed)
    plane, tall = rows * frames, row_dev * frames
    for w in range(cols):
        here = pl.multiple_of(w * plane + lax.axis_index("rows") * tall, frames)
        acc_ref[pl.ds(here, tall), :] *= own_ref[w * tall : (w + 1) * tall, :]


def second_kernel(dims, cols_all, *refs):
    time_devs, row_devs, frame_dev, row_dev, col_dev = dims
    pieces, acc_ref, mid_ref, weight_ref, out_ref = refs[:row_devs], *refs[row_devs : row_devs + 4]
    slopes, full, grad, *shifts = refs[row_devs + 4 :]
    frames, rows = time_devs * frame_dev, row_devs * row_dev
    plane, pitch, tall = rows * frames, (rows + 2) * frames, row_dev * frames
    sizes = window_rows((1, 0), tall, col_dev)
    sources = row_sources(row_devs)
    first_col = (lax.axis_index("tm") * row_devs + lax.axis_index("rows")) * col_dev - 1

    def slope(at, begin, lane):
        value = pieces[at][begin : begin + tall, lane]
        return value if at == 0 else silu_slope(value.astype(F32))

    for w in range(col_dev + 2):
        col = first_col + w
        inside = jnp.logical_and(col >= 0, col < cols_all)
        edge = jnp.zeros((full.shape[0], frames, LANES), F32)
        full[:, w * pitch : w * pitch + frames, :] = edge
        full[:, (w + 1) * pitch - frames : (w + 1) * pitch, :] = edge
        for at, source in enumerate(sources):
            here = pl.multiple_of(w * plane + source * tall, frames)
            start = pl.multiple_of(w * pitch + frames + source * tall, frames)
            for at_lane, lane in lanes(acc_ref.shape[1]):
                value = acc_ref[pl.ds(here, tall), lane]
                if at:
                    value = value * slope(at, w * tall, lane)
                full[at_lane, pl.ds(start, tall), :] = jnp.where(inside, value, 0.0)
    full[:, (col_dev + 2) * pitch :, :] = jnp.zeros((full.shape[0], frames, LANES), F32)
    for w in range(col_dev):
        for at, source in enumerate(sources):
            here = pl.multiple_of(w * plane + source * tall, frames)
            for at_lane, lane in lanes(acc_ref.shape[1]):
                slopes[at_lane, pl.ds(here, tall), :] = slope(at, sizes[1] + w * tall, lane)
    for a in range(3):
        spread(full, shifts[a], a, col_dev + 2, rows, frames)
        moved, mixed = taps_of(shifts[a], weight_ref.at[2 - a], col_dev, rows, frames)
        part = dot_last(mixed, moved)
        grad[...] = grad[...] + part if a else part
    size = col_dev * plane
    for at_lane, lane in lanes(grad.shape[0]):
        full[at_lane, 0:size, :] = mid_ref[at_lane] + grad[lane, :].T * slopes[at_lane]
        for frame in range(frames):
            for row in range(rows):
                out_ref[0, frame, row, :, lane] = full[
                    at_lane, pl.ds(row * frames + frame, col_dev, stride=plane), :
                ]


def kernel_call(body, out_shape, in_specs, scratch, flops, room=24):
    return pl.pallas_call(
        body,
        out_shape=out_shape,
        in_specs=in_specs,
        out_specs=jax.tree.map(lambda _: VMEM, out_shape),
        scratch_shapes=scratch,
        compiler_params=pltpu.CompilerParams(vmem_limit_bytes=room << 20),
        cost_estimate=pl.CostEstimate(flops=flops, bytes_accessed=4 << 20, transcendentals=0),
    )


def on_device(latents, hidden, cotangent, conv_one, conv_two, lengths):
    _, frame_dev, row_dev, cols, channels = latents.shape
    time_devs, row_devs = lax.axis_size("tm"), lax.axis_size("rows")
    col_dev = cols // (time_devs * row_devs)
    frames, rows = time_devs * frame_dev, row_devs * row_dev
    dims = (time_devs, row_devs, frame_dev, row_dev, col_dev)
    plane, pitch = rows * frames, (rows + 2) * frames
    parts = channels // LANES

    def over_tm(windows):
        out = [windows[0]]
        for step, (pairs, _, _) in enumerate(pairing(time_devs)):
            out.append(lax.ppermute(windows[step + 1], "tm", pairs))
        return out

    def over_rows(pieces):
        out = []
        for at, (pairs, _, _) in enumerate(pairing(row_devs)):
            out.append(lax.ppermute(pieces[at], "rows", pairs))
        return out

    def for_rows(windows, halos, slopes):
        sent = []
        if row_devs > 1:
            sent = share(dims, halos, False, False, windows)
        own = share(dims, halos, True, slopes, windows)
        return [*own, *over_rows(sent)]

    def part_rows(size):
        return pltpu.VMEM((parts, size, LANES), F32)

    mac = 2 * 9 * channels * channels
    wide, narrow = (col_dev + 2) * plane, col_dev * plane
    cot = pack([cotangent[0]], lengths, (2,), True, time_devs)
    cot = for_rows(over_tm(cot), (2,), False)
    hid = pack([hidden[0], latents[0]], lengths, (1, 0), False, time_devs)
    hid = for_rows(over_tm(hid), (1, 0), True)
    acc, mid, moved = kernel_call(
        functools.partial(first_kernel, dims),
        [
            jax.ShapeDtypeStruct((wide, channels), F32),
            jax.ShapeDtypeStruct((parts, narrow, LANES), F32),
            jax.ShapeDtypeStruct((2, (col_dev + 4) * pitch, channels), BF16),
        ],
        [VMEM] * (row_devs + 1),
        [
            part_rows((col_dev + 4) * pitch + frames),
            *[pltpu.VMEM((2, (col_dev + 4) * pitch, channels), BF16)] * 2,
        ],
        3 * mac * wide,
    )(*cot, conv_two)
    acc = kernel_call(
        functools.partial(last_tap_kernel, dims, col_dev + 2),
        jax.ShapeDtypeStruct((wide, channels), F32),
        [VMEM] * 4,
        [],
        mac * wide,
    )(acc, moved, conv_two, hid[0])
    return kernel_call(
        functools.partial(second_kernel, dims, cols),
        jax.ShapeDtypeStruct((1, frames, rows, col_dev, channels), F32),
        [VMEM] * (row_devs + 3),
        [
            part_rows(narrow),
            part_rows((col_dev + 2) * pitch + frames),
            pltpu.VMEM((channels, narrow), F32),
            *[pltpu.VMEM((2, (col_dev + 2) * pitch, channels), BF16)] * 3,
        ],
        3 * mac * narrow,
    )(*hid, acc, mid, conv_one)


def solution(mesh):
    spec = P("dp", "tm", "rows", None, None)
    return jax.shard_map(
        on_device,
        mesh=mesh,
        in_specs=(spec, spec, spec, P(), P(), P("dp")),
        out_specs=P("dp", None, None, ("tm", "rows"), None),
        check_vma=False,
    )
```
